512 devices in a mesh: rep: 128 (over x, z, core), tp: 4 (over y).
Axes of the slice: x: 4, y: 4, z: 16, core: 2. Of those that a mesh axis runs over, the one named last changes fastest.
Arguments:
- tokens: bfloat16 [16384, 1024], P('rep', 'tp'), may hold values from -6 to 6
- attn_gain: float32 [1024], replicated, may hold values from 0.1 to 1.9
- ffn_gain: float32 [1024], replicated, may hold values from 0.1 to 1.9
- w_query: bfloat16 [1024, 1024], P(None, 'tp'), may hold values from -0.0625 to 0.0625
- w_key: bfloat16 [1024, 1024], P(None, 'tp'), may hold values from -0.1875 to 0.1875
- w_value: bfloat16 [1024, 1024], P(None, 'tp'), may hold values from -0.1875 to 0.1875
- w_out: bfloat16 [1024, 1024], P('tp'), may hold values from -0.1875 to 0.1875
- w_inner: bfloat16 [1024, 2048], P(None, 'tp'), may hold values from -0.1875 to 0.1875
- w_outer: bfloat16 [2048, 1024], P('tp'), may hold values from -0.125 to 0.125
- bias_table: float32 [32, 16], P(None, 'tp'), may hold values from -3 to 3
- cache_keys: bfloat16 [256, 64, 1024], P('rep', None, 'tp'), may hold values from -68 to 68
- cache_values: bfloat16 [256, 64, 1024], P('rep', None, 'tp'), may hold values from -6 to 6
- new_counts: int32 [2, 128], P(None, 'rep'), may hold values from 1 to 64, 4096 in all within a row
- cached_lengths: int32 [2, 128], P(None, 'rep'), may hold values from 1 to 64, 4096 in all within a row
- deal: int32 [128, 128], P('rep'), may hold values from 0 to 127, each once within a row
Outputs:
- dealt: bfloat16 [16384, 1024], P('rep', 'tp')
The draws below stay inside these ranges and needn't reach their ends.
Inputs may be any that keep to these rules, and one draw needn't show every extreme that they name: `new_counts`: for each j the counts over the replicas sum to 4096. `cached_lengths`: for each j the lengths over the replicas sum to 4096. `deal`: each row holds every number of 0 to 127 once.
All inputs are finite; a program needn't handle non-finite values. No bound on the sum of `new_counts` or of `cached_lengths` on one device may be relied on, other than what follows from the above.
Results may differ from the reference program's by a relative error of at most 0.013.
The reference program's roundings to bfloat16 on the way (of `normed`, `attn_probs`, `context`, `ffn_input`, `hidden` and `layer_out`) count: a program that leaves them out, or rounds other values in their place, can miss the bound.
Values may be sent and summed in bfloat16 or wider, within the bound.
A program may use at most 64 MiB of HBM per device.

```python
import math
import jax
import jax.numpy as jnp
import numpy as np
from jax import lax

D = 1024
HEADS = 16
HDIM = 64
FF = 2048
BUCKETS = 32
REQ_DEV = 2
QLEN = 64
CLEN = 64
TOK_DEV = 128
REQS = 256
TOKENS = 16384
N_REP = 128


def draw_cache_keys(key, part):
    first = jax.random.fold_in(key, 0)
    base = jnp.clip(jax.random.normal(first, (REQS, CLEN, D), jnp.float32), -4.0, 4.0)
    return base.astype(jnp.bfloat16)


def steps_of(rng, extent, pieces, low, top_value):
    def one(axis_at, blocks):
        draws = jax.random.uniform(jax.random.fold_in(jax.random.fold_in(rng, 6), axis_at), (blocks,), jnp.float32, low / len(pieces), top_value / len(pieces))
        return jnp.repeat(jnp.exp(draws), extent[axis_at] // blocks).reshape((-1,) + (1,) * (len(extent) - axis_at - 1))

    gain = one(*pieces[0])
    for cut in pieces[1:]:
        gain = gain * one(*cut)
    return gain


def split_up(amount, total, bound, skew):
    loads = [(1 << 20) // math.isqrt(rank ** skew) + 1 for rank in range(2, amount + 1)]
    spare, holding = total - bound - (amount - 1), [1] * (amount - 1)
    while spare > 0:
        free = [i for i in range(amount - 1) if holding[i] < bound]
        pool, budget = sum([loads[i] for i in free]), spare
        for i in free:
            more = min(bound - holding[i], max(1, budget * loads[i] // pool), spare)
            holding[i] = holding[i] + more
            spare = spare - more
    return np.array([bound] + holding)


def uneven(key, amount, total, limit, skew):
    if amount == 2:
        one = jax.random.randint(key, (), max(1, total - limit), min(limit, total - 1) + 1)
        return jnp.stack([one, total - one])
    tallies = jnp.asarray(split_up(amount, total, limit, skew), jnp.int32)
    couples = (amount - 1) // 2
    source_of, sink = tallies[1:1 + 2 * couples:2], tallies[2:2 + 2 * couples:2]
    margin = jnp.minimum(source_of - 1, limit - sink)
    shifted = jax.random.randint(jax.random.fold_in(key, 1), (couples,), 0, 1 << 20) % (margin + 1)
    tallies = tallies.at[1:1 + 2 * couples:2].set(source_of - shifted).at[2:2 + 2 * couples:2].set(sink + shifted)
    return tallies[jax.random.permutation(jax.random.fold_in(key, 2), amount)]


def gaussian(key, extent, spread, reach, cuts=(), held_as=jnp.bfloat16):
    gain = steps_of(key, extent, cuts, -0.22, 0.18) if cuts else 1.0
    entries = jax.random.normal(key, extent, jnp.float32) * spread * gain
    return jnp.minimum(jnp.maximum(entries, -reach), reach).astype(held_as)


def setup_inputs(seed: int = 0) -> dict:
    keys = jax.random.split(jax.random.key(seed), 16)
    tokens = gaussian(keys[0], (TOKENS, D), 1.0, 6.0, ((0, 128), (1, 4)))
    attn_gain = jnp.clip(1.0 + 0.18 * jax.random.normal(keys[1], (D,), jnp.float32), 0.1, 1.9)
    ffn_gain = jnp.clip(1.0 + 0.18 * jax.random.normal(keys[2], (D,), jnp.float32), 0.1, 1.9)
    w_query = gaussian(keys[3], (D, D), (8 * D) ** -0.5, 0.0625, ((1, 4),))
    w_key = gaussian(keys[4], (D, D), D ** -0.5, 0.1875, ((1, 4),))
    w_value = gaussian(keys[5], (D, D), D ** -0.5, 0.1875, ((1, 4),))
    w_out = gaussian(keys[6], (D, D), D ** -0.5, 0.1875, ((0, 4),))
    w_inner = gaussian(keys[7], (D, FF), D ** -0.5, 0.1875, ((1, 4),))
    w_outer = gaussian(keys[8], (FF, D), FF ** -0.5, 0.125, ((0, 4),))
    bias_table = jnp.clip(jax.random.uniform(keys[9], (BUCKETS, HEADS), jnp.float32, -3.0, 3.0) * steps_of(keys[9], (BUCKETS, HEADS), ((1, 4),), -0.4, 0.0), -3.0, 3.0)
    cache_keys = draw_cache_keys(jax.random.fold_in(keys[15], 71), 0)
    cache_values = gaussian(keys[11], (REQS, CLEN, D), 1.0, 6.0, ((0, 128), (2, 4)))
    new_counts = jax.vmap(lambda own: uneven(own, N_REP, N_REP * QLEN // 2, QLEN, 2))(jax.random.split(keys[12], REQ_DEV)).reshape((REQ_DEV, N_REP)).astype(jnp.int32)
    cached_lengths = jax.vmap(lambda own: uneven(own, N_REP, N_REP * CLEN // 2, CLEN, 2))(jax.random.split(keys[13], REQ_DEV)).reshape((REQ_DEV, N_REP)).astype(jnp.int32)
    deal = jax.vmap(lambda own: jax.random.permutation(own, TOK_DEV))(jax.random.split(keys[14], N_REP)).reshape((N_REP, TOK_DEV)).astype(jnp.int32)
    return dict(tokens=tokens, attn_gain=attn_gain, ffn_gain=ffn_gain, w_query=w_query, w_key=w_key, w_value=w_value, w_out=w_out, w_inner=w_inner, w_outer=w_outer, bias_table=bias_table, cache_keys=cache_keys, cache_values=cache_values, new_counts=new_counts, cached_lengths=cached_lengths, deal=deal)


EPSILON = 1e-06
THRESHOLDS = (12, 16, 23, 32, 46, 64, 91)

def bucket_of(relative):
    distance = jnp.abs(relative)
    larger = 8 + sum(((distance >= threshold).astype(jnp.int32) for threshold in THRESHOLDS))
    near = jnp.where(distance < 8, distance, larger)
    return near + 16 * (relative > 0).astype(jnp.int32)

def rms_scale(values):
    return lax.rsqrt(lax.optimization_barrier(jnp.mean(values * values, axis=-1, keepdims=True)) + EPSILON)

def reference(tokens, attn_gain, ffn_gain, w_query, w_key, w_value, w_out, w_inner, w_outer, bias_table, cache_keys, cache_values, new_counts, cached_lengths, deal):
    stream = tokens.astype(jnp.float32)
    normed = (stream * rms_scale(stream) * attn_gain).astype(jnp.bfloat16)
    queries = jnp.dot(normed, w_query, preferred_element_type=jnp.float32).astype(jnp.bfloat16).reshape(REQS, QLEN, HEADS, HDIM)
    new_keys = jnp.dot(normed, w_key, preferred_element_type=jnp.float32).astype(jnp.bfloat16).reshape(REQS, QLEN, D)
    new_values = jnp.dot(normed, w_value, preferred_element_type=jnp.float32).astype(jnp.bfloat16).reshape(REQS, QLEN, D)
    counts = new_counts.T.reshape(REQS).astype(jnp.int32)
    lengths = cached_lengths.T.reshape(REQS).astype(jnp.int32)
    key_index = jnp.arange(CLEN + QLEN, dtype=jnp.int32)
    offsets = jnp.arange(QLEN, dtype=jnp.int32)
    per_head = bias_table.T

    def attend(item):
        query, cache_k, cache_v, fresh_k, fresh_v, count, length = item
        all_keys = jnp.concatenate([cache_k, fresh_k], axis=0).reshape(CLEN + QLEN, HEADS, HDIM).astype(jnp.float32)
        all_values = jnp.concatenate([cache_v, fresh_v], axis=0).reshape(CLEN + QLEN, HEADS, HDIM).astype(jnp.float32)
        scores = jnp.einsum('qhd,khd->hqk', query.astype(jnp.float32), all_keys)
        is_cache = key_index < CLEN
        key_position = jnp.where(is_cache, key_index, length + key_index - CLEN)
        relative = key_position[None, :] - (length + offsets)[:, None]
        rel_bias = jnp.take(per_head, bucket_of(relative), axis=1)
        live_key = jnp.where(is_cache, key_index < length, key_index - CLEN < count)
        scores = jnp.where(live_key[None, None, :], scores + rel_bias, -1e+30)
        row_max = lax.optimization_barrier(jnp.max(scores, axis=2, keepdims=True))
        weights = jnp.exp(scores - row_max)
        attn_probs = (weights / lax.optimization_barrier(jnp.sum(weights, axis=2, keepdims=True))).astype(jnp.bfloat16)
        context = jnp.einsum('hqk,khd->qhd', attn_probs.astype(jnp.float32), all_values)
        return context.astype(jnp.bfloat16).reshape(QLEN, D)
    context = lax.map(attend, (queries, cache_keys, cache_values, new_keys, new_values, counts, lengths)).reshape(TOKENS, D)
    mixed = stream + jnp.dot(context, w_out, preferred_element_type=jnp.float32)
    live_rows = (offsets[None, :] < counts[:, None]).reshape(TOKENS, 1)
    mixed = jnp.where(live_rows, mixed, 0.0)
    ffn_input = (mixed * rms_scale(mixed) * ffn_gain).astype(jnp.bfloat16)
    hidden = jnp.maximum(jnp.dot(ffn_input, w_inner, preferred_element_type=jnp.float32), 0.0).astype(jnp.bfloat16)
    layer_out = (mixed + jnp.dot(hidden, w_outer, preferred_element_type=jnp.float32)).astype(jnp.bfloat16)
    replicas = jnp.arange(N_REP, dtype=jnp.int32)
    target = deal % N_REP * TOK_DEV + replicas[:, None] * (TOK_DEV // N_REP) + deal // N_REP
    return jnp.zeros_like(layer_out).at[target.reshape(TOKENS)].set(layer_out)
```

```python
import jax
import jax.numpy as jnp
from jax import lax
from jax.experimental import pallas as pl
from jax.experimental.pallas import tpu as pltpu
from jax.sharding import PartitionSpec as P

EPSILON = 1e-06
THRESHOLDS = (12, 16, 23, 32, 46, 64, 91)
BUCKETS = 32
TP = 4
SIDES = 8
DEPTH = 16
MESH = pl.DeviceIdType.MESH
BF16 = jnp.bfloat16
F32 = jnp.float32


def iota(shape, dim):
    return lax.broadcasted_iota(jnp.int32, shape, dim)


def dot(a, b):
    return jnp.dot(a, b, preferred_element_type=F32)


def dot_t(a, b):
    return lax.dot_general(a, b, (((1,), (1,)), ((), ())), preferred_element_type=F32)


def bucket_of(relative):
    distance = jnp.abs(relative)
    larger = 8 + sum(((distance >= threshold).astype(jnp.int32) for threshold in THRESHOLDS))
    near = jnp.where(distance < 8, distance, larger)
    return near + 16 * (relative > 0).astype(jnp.int32)


def one_hot(condition):
    return jnp.where(condition, 1.0, 0.0).astype(BF16)


def kernel(
    tokens_ref,
    attn_gain_ref,
    ffn_gain_ref,
    w_query_ref,
    w_key_ref,
    w_value_ref,
    w_out_ref,
    w_inner_ref,
    w_outer_ref,
    bias_ref,
    cache_k_ref,
    cache_v_ref,
    counts_ref,
    lengths_ref,
    deal_ref,
    out_ref,
    x_full,
    w_qkv,
    w_out,
    w_inner,
    w_outer,
    cache_k,
    cache_v,
    bias,
    partial,
    send_rows,
    recv_rows,
    ffn_full,
    send_cols,
    recv_cols,
    side_send,
    side_recv,
    z_send,
    z_recv,
    load_sem,
    ag_send,
    ag_recv,
    rs_send,
    rs_recv,
    ag2_send,
    ag2_recv,
    rs2_send,
    rs2_recv,
    side_send_sem,
    side_recv_sem,
    z_send_sem,
    z_recv_sem,
):
    rep = lax.axis_index("rep")
    tp = lax.axis_index("tp")
    tokens, width = tokens_ref.shape
    model = w_qkv.shape[0]
    requests, cached, _ = cache_k_ref.shape
    slots = tokens // requests
    heads = bias_ref.shape[1]
    hdim = width // heads
    keys = cached + slots
    own = tokens // TP
    x_at, z_at, core = rep // (2 * DEPTH), (rep // 2) % DEPTH, rep % 2
    side = x_at * 2 + core

    def tp_peer(offset):
        return (tp + offset) % TP

    def side_peer(offset):
        other = (side + offset) % SIDES
        return other, (other // 2) * (2 * DEPTH) + z_at * 2 + other % 2

    def z_peer(offset):
        other = (z_at + offset) % DEPTH
        return other, x_at * (2 * DEPTH) + other * 2 + core

    barrier = pltpu.get_barrier_semaphore()
    for offset in range(1, TP):
        pl.semaphore_signal(barrier, inc=1, device_id={"tp": tp_peer(offset)}, device_id_type=MESH)
    for offset in range(1, SIDES):
        pl.semaphore_signal(barrier, inc=1, device_id={"rep": side_peer(offset)[1]}, device_id_type=MESH)
    for offset in range(1, DEPTH):
        pl.semaphore_signal(barrier, inc=1, device_id={"rep": z_peer(offset)[1]}, device_id_type=MESH)

    own_cols = pl.ds(pl.multiple_of(tp * width, width), width)
    own_rows = pl.ds(pl.multiple_of(tp * own, own), own)

    loads = [
        pltpu.make_async_copy(src, dst, load_sem.at[i])
        for i, (src, dst) in enumerate(
            [
                (tokens_ref, x_full.at[:, own_cols]),
                (w_query_ref, w_qkv.at[:, pl.ds(0, width)]),
                (w_key_ref, w_qkv.at[:, pl.ds(width, width)]),
                (w_value_ref, w_qkv.at[:, pl.ds(2 * width, width)]),
                (cache_k_ref, cache_k),
                (cache_v_ref, cache_v),
                (w_out_ref, w_out),
                (w_inner_ref, w_inner),
                (w_outer_ref, w_outer),
            ]
        )
    ]
    for load in loads:
        load.start()

    pl.semaphore_wait(barrier, (TP - 1) + (SIDES - 1) + (DEPTH - 1))

    loads[0].wait()
    gathers = []
    for offset in (2, 1, 3):
        copy = pltpu.make_async_remote_copy(
            src_ref=x_full.at[:, own_cols],
            dst_ref=x_full.at[:, own_cols],
            send_sem=ag_send.at[offset - 1],
            recv_sem=ag_recv.at[offset - 1],
            device_id={"tp": tp_peer(offset)},
            device_id_type=MESH,
        )
        copy.start()
        gathers.append(copy)

    key = iota((slots, keys), 1)
    query = iota((slots, keys), 0)
    for r in range(requests):
        length = lengths_ref[r, 0]
        position = jnp.where(key < cached, key, length + key - cached)
        bucket = bucket_of(position - (length + query))
        rows = [jnp.zeros((slots, keys), F32) for _ in range(heads)]
        for b in range(BUCKETS):
            here = bucket == b
            rows = [jnp.where(here, bias_ref[b, h], rows[h]) for h in range(heads)]
        for h in range(heads):
            bias[r, pl.ds(h * slots, slots), :] = rows[h]

    q_row = iota((tokens, tokens), 0)
    k_col = iota((tokens, tokens), 1)
    q_side, q_z = q_row // DEPTH, q_row % DEPTH
    destination = (q_side // 2) * (2 * DEPTH) + q_z * 2 + q_side % 2
    count_of = jnp.where(k_col // slots == 0, counts_ref[0, 0], counts_ref[requests - 1, 0])
    live = (k_col % slots) < count_of
    order = jnp.where((deal_ref[...] == destination) & live, 1.0, 0.0)

    for copy in gathers:
        copy.wait_recv()

    stream = x_full[...].astype(F32)
    inverse = lax.rsqrt(jnp.mean(stream * stream, axis=1, keepdims=True) + EPSILON)
    normed = (stream * inverse * attn_gain_ref[...]).astype(BF16)
    for load in loads[1:4]:
        load.wait()
    qkv = dot(normed, w_qkv[...]).astype(BF16)

    loads[4].wait()
    loads[5].wait()
    lane_head = iota((slots, width), 1) // hdim
    key_row = iota((heads * slots, keys), 1)
    contexts = []
    for r in range(requests):
        rows = slice(r * slots, (r + 1) * slots)
        queries = qkv[rows, 0:width]
        all_keys = jnp.concatenate([cache_k[r], qkv[rows, width : 2 * width]], axis=0)
        all_values = jnp.concatenate([cache_v[r], qkv[rows, 2 * width :]], axis=0)
        stacked = jnp.concatenate(
            [jnp.where(lane_head == h, queries, jnp.zeros_like(queries)) for h in range(heads)], axis=0
        )
        scores = dot_t(stacked, all_keys) + bias[r]
        limit = jnp.where(key_row < cached, lengths_ref[r, 0], cached + counts_ref[r, 0])
        scores = jnp.where(key_row < limit, scores, -1e30)
        weights = jnp.exp(scores - jnp.max(scores, axis=1, keepdims=True))
        probs = (weights / jnp.sum(weights, axis=1, keepdims=True)).astype(BF16)
        spread = dot(probs, all_values)
        context = jnp.zeros((slots, width), F32)
        for h in range(heads):
            context = jnp.where(lane_head == h, spread[h * slots : (h + 1) * slots], context)
        contexts.append(context.astype(BF16))
    context = jnp.concatenate(contexts, axis=0)

    moved = dot(order.astype(BF16), context).astype(BF16)
    loads[6].wait()
    partial[...] = dot(moved, w_out[...])
    send_rows[...] = partial[...].astype(BF16)
    row_sends = []
    for offset in (2, 1, 3):
        peer = tp_peer(offset)
        copy = pltpu.make_async_remote_copy(
            src_ref=send_rows.at[pl.ds(pl.multiple_of(peer * own, own), own), :],
            dst_ref=recv_rows.at[offset - 1],
            send_sem=rs_send.at[offset - 1],
            recv_sem=rs_recv.at[offset - 1],
            device_id={"tp": peer},
            device_id_type=MESH,
        )
        copy.start()
        row_sends.append(copy)

    own_q = iota((own, tokens), 0) + tp * own
    own_k = iota((own, tokens), 1)
    own_side, own_z = own_q // DEPTH, own_q % DEPTH
    own_destination = (own_side // 2) * (2 * DEPTH) + own_z * 2 + own_side % 2
    own_count = jnp.where(own_k // slots == 0, counts_ref[0, 0], counts_ref[requests - 1, 0])
    own_order = one_hot((deal_ref[...] == own_destination) & ((own_k % slots) < own_count))
    mixed = dot(own_order, x_full[...]) + partial[own_rows, :]

    for copy in row_sends:
        copy.wait_recv()
    mixed = mixed + (recv_rows[0].astype(F32) + recv_rows[1].astype(F32) + recv_rows[2].astype(F32))
    inverse_ffn = lax.rsqrt(jnp.mean(mixed * mixed, axis=1, keepdims=True) + EPSILON)
    ffn_full[own_rows, :] = (mixed * inverse_ffn * ffn_gain_ref[...]).astype(BF16)
    ffn_gathers = []
    for offset in (2, 1, 3):
        copy = pltpu.make_async_remote_copy(
            src_ref=ffn_full.at[own_rows, :],
            dst_ref=ffn_full.at[own_rows, :],
            send_sem=ag2_send.at[offset - 1],
            recv_sem=ag2_recv.at[offset - 1],
            device_id={"tp": tp_peer(offset)},
            device_id_type=MESH,
        )
        copy.start()
        ffn_gathers.append(copy)
    loads[7].wait()
    loads[8].wait()
    for copy in ffn_gathers:
        copy.wait_recv()

    hidden = jnp.maximum(dot(ffn_full[...], w_inner[...]), 0.0).astype(BF16)
    partial[...] = dot(hidden, w_outer[...])
    partial[own_rows, :] = partial[own_rows, :] + mixed
    send_cols[...] = partial[...].astype(BF16)
    col_sends = []
    for offset in (2, 1, 3):
        peer = tp_peer(offset)
        copy = pltpu.make_async_remote_copy(
            src_ref=send_cols.at[:, pl.ds(pl.multiple_of(peer * width, width), width)],
            dst_ref=recv_cols.at[offset - 1],
            send_sem=rs2_send.at[offset - 1],
            recv_sem=rs2_recv.at[offset - 1],
            device_id={"tp": peer},
            device_id_type=MESH,
        )
        copy.start()
        col_sends.append(copy)
    to_row = iota((2 * tokens, 2 * tokens), 0)
    to_col = iota((2 * tokens, 2 * tokens), 1)
    gather_z = one_hot(
        to_col
        == ((to_row // SIDES) % 2) * tokens + (to_row % SIDES) * DEPTH + to_row // (2 * SIDES)
    )
    final = partial[:, own_cols]
    for copy in col_sends:
        copy.wait_recv()
    final = final + (recv_cols[0].astype(F32) + recv_cols[1].astype(F32) + recv_cols[2].astype(F32))
    side_send[...] = final.astype(BF16).reshape(SIDES, DEPTH, width)

    side_sends = []
    for offset in range(1, SIDES):
        other, peer = side_peer(offset)
        copy = pltpu.make_async_remote_copy(
            src_ref=side_send.at[other],
            dst_ref=side_recv.at[side],
            send_sem=side_send_sem.at[offset - 1],
            recv_sem=side_recv_sem.at[offset - 1],
            device_id={"rep": peer},
            device_id_type=MESH,
        )
        copy.start()
        side_sends.append(copy)
    side_recv[side] = side_send[side]
    d_row = iota((tokens, 2 * tokens), 0)
    d_col = iota((tokens, 2 * tokens), 1)
    d_from = ((d_row // 2) % DEPTH) * (2 * SIDES) + (d_row // (2 * DEPTH)) * 2 + d_row % 2
    left = one_hot(d_col == d_from)
    right = one_hot(d_col == d_from + SIDES)
    for copy in side_sends:
        copy.wait_recv()

    arrived = side_recv[...].reshape(tokens, width)
    halves = jnp.concatenate([arrived[:, : width // 2], arrived[:, width // 2 :]], axis=0)
    z_send[...] = dot(gather_z, halves).astype(BF16).reshape(DEPTH, 2 * SIDES, width // 2)
    z_sends = []
    for offset in range(1, DEPTH):
        other, peer = z_peer(offset)
        copy = pltpu.make_async_remote_copy(
            src_ref=z_send.at[other],
            dst_ref=z_recv.at[z_at],
            send_sem=z_send_sem.at[offset - 1],
            recv_sem=z_recv_sem.at[offset - 1],
            device_id={"rep": peer},
            device_id_type=MESH,
        )
        copy.start()
        z_sends.append(copy)
    z_recv[z_at] = z_send[z_at]
    for copy in gathers + row_sends + ffn_gathers + col_sends + side_sends:
        copy.wait_send()
    for copy in z_sends:
        copy.wait_recv()
    landed = z_recv[...].reshape(2 * tokens, width // 2)
    out_ref[:, : width // 2] = dot(left, landed).astype(BF16)
    out_ref[:, width // 2 :] = dot(right, landed).astype(BF16)
    for copy in z_sends:
        copy.wait_send()


def on_device(
    tokens,
    attn_gain,
    ffn_gain,
    w_query,
    w_key,
    w_value,
    w_out,
    w_inner,
    w_outer,
    bias_table,
    cache_keys,
    cache_values,
    new_counts,
    cached_lengths,
    deal,
):
    rows, width = tokens.shape
    model = w_query.shape[0]
    ff = w_inner.shape[1]
    requests, cached, _ = cache_keys.shape
    slots = rows // requests
    heads = bias_table.shape[1]
    own = rows // TP
    hbm = pl.BlockSpec(memory_space=pltpu.HBM)
    vmem = pl.BlockSpec(memory_space=pltpu.VMEM)
    smem = pl.BlockSpec(memory_space=pltpu.SMEM)
    dma = pltpu.SemaphoreType.DMA
    return pl.pallas_call(
        kernel,
        out_shape=jax.ShapeDtypeStruct((rows, width), BF16),
        in_specs=[
            hbm, vmem, vmem, hbm, hbm, hbm, hbm, hbm, hbm, smem, hbm, hbm, smem, smem, vmem,
        ],
        out_specs=vmem,
        scratch_shapes=[
            pltpu.VMEM((rows, model), BF16),
            pltpu.VMEM((model, 3 * width), BF16),
            pltpu.VMEM((width, model), BF16),
            pltpu.VMEM((model, ff), BF16),
            pltpu.VMEM((ff, model), BF16),
            pltpu.VMEM((requests, cached, width), BF16),
            pltpu.VMEM((requests, cached, width), BF16),
            pltpu.VMEM((requests, heads * slots, cached + slots), F32),
            pltpu.VMEM((rows, model), F32),
            pltpu.VMEM((rows, model), BF16),
            pltpu.VMEM((TP - 1, own, model), BF16),
            pltpu.VMEM((rows, model), BF16),
            pltpu.VMEM((rows, model), BF16),
            pltpu.VMEM((TP - 1, rows, width), BF16),
            pltpu.VMEM((SIDES, DEPTH, width), BF16),
            pltpu.VMEM((SIDES, DEPTH, width), BF16),
            pltpu.VMEM((DEPTH, 2 * SIDES, width // 2), BF16),
            pltpu.VMEM((DEPTH, 2 * SIDES, width // 2), BF16),
            dma((9,)),
            dma((TP - 1,)),
            dma((TP - 1,)),
            dma((TP - 1,)),
            dma((TP - 1,)),
            dma((TP - 1,)),
            dma((TP - 1,)),
            dma((TP - 1,)),
            dma((TP - 1,)),
            dma((SIDES - 1,)),
            dma((SIDES - 1,)),
            dma((DEPTH - 1,)),
            dma((DEPTH - 1,)),
        ],
        compiler_params=pltpu.CompilerParams(
            collective_id=0, has_side_effects=True, vmem_limit_bytes=40 * 1024 * 1024
        ),
    )(
        tokens,
        attn_gain.reshape(1, model),
        ffn_gain.reshape(1, model),
        w_query,
        w_key,
        w_value,
        w_out,
        w_inner,
        w_outer,
        bias_table,
        cache_keys,
        cache_values,
        new_counts,
        cached_lengths,
        deal,
    )


def solution(mesh):
    in_specs = (
        P("rep", "tp"),
        P(),
        P(),
        P(None, "tp"),
        P(None, "tp"),
        P(None, "tp"),
        P("tp", None),
        P(None, "tp"),
        P("tp", None),
        P(None, "tp"),
        P("rep", None, "tp"),
        P("rep", None, "tp"),
        P(None, "rep"),
        P(None, "rep"),
        P("rep", None),
    )
    out_specs = P("rep", "tp")
    return jax.shard_map(
        on_device, mesh=mesh, in_specs=in_specs, out_specs=out_specs, check_vma=False
    )
```

```python
import jax
import jax.numpy as jnp
from jax import lax
from jax.experimental import pallas as pl
from jax.experimental.pallas import tpu as pltpu
from jax.sharding import PartitionSpec as P

EPSILON = 1e-06
THRESHOLDS = (12, 16, 23, 32, 46, 64, 91)
BUCKETS = 32
TP = 4
SIDES = 8
DEPTH = 16
MESH = pl.DeviceIdType.MESH
BF16 = jnp.bfloat16
F32 = jnp.float32


def iota(shape, dim):
    return lax.broadcasted_iota(jnp.int32, shape, dim)


def dot(a, b):
    return jnp.dot(a, b, preferred_element_type=F32)


def dot_t(a, b):
    return lax.dot_general(a, b, (((1,), (1,)), ((), ())), preferred_element_type=F32)


def bucket_of(relative):
    distance = jnp.abs(relative)
    larger = 8 + sum(((distance >= threshold).astype(jnp.int32) for threshold in THRESHOLDS))
    near = jnp.where(distance < 8, distance, larger)
    return near + 16 * (relative > 0).astype(jnp.int32)


def one_hot(condition):
    return jnp.where(condition, 1.0, 0.0).astype(BF16)


def kernel(
    tokens_ref,
    attn_gain_hbm,
    ffn_gain_hbm,
    w_query_ref,
    w_key_ref,
    w_value_ref,
    w_out_ref,
    w_inner_ref,
    w_outer_ref,
    bias_hbm,
    cache_k_ref,
    cache_v_ref,
    counts_hbm,
    lengths_hbm,
    deal_hbm,
    out_ref,
    attn_gain_ref,
    ffn_gain_ref,
    bias_ref,
    counts_ref,
    lengths_ref,
    deal_ref,
    x_full,
    w_qkv,
    w_out,
    w_inner,
    w_outer,
    cache_k,
    cache_v,
    bias,
    partial,
    send_rows,
    recv_rows,
    ffn_full,
    send_cols,
    recv_cols,
    side_send,
    side_recv,
    z_send,
    z_recv,
    load_sem,
    ag_send,
    ag_recv,
    rs_send,
    rs_recv,
    ag2_send,
    ag2_recv,
    rs2_send,
    rs2_recv,
    side_send_sem,
    side_recv_sem,
    z_send_sem,
    z_recv_sem,
):
    rep = lax.axis_index("rep")
    tp = lax.axis_index("tp")
    tokens, width = tokens_ref.shape
    model = w_qkv.shape[0]
    requests, cached, _ = cache_k_ref.shape
    slots = tokens // requests
    heads = bias_ref.shape[0]
    hdim = width // heads
    keys = cached + slots
    own = tokens // TP
    x_at, z_at, core = rep // (2 * DEPTH), (rep // 2) % DEPTH, rep % 2
    side = x_at * 2 + core

    def tp_peer(offset):
        return (tp + offset) % TP

    def side_peer(offset):
        other = (side + offset) % SIDES
        return other, (other // 2) * (2 * DEPTH) + z_at * 2 + other % 2

    def z_peer(offset):
        other = (z_at + offset) % DEPTH
        return other, x_at * (2 * DEPTH) + other * 2 + core

    barrier = pltpu.get_barrier_semaphore()
    for offset in range(1, TP):
        pl.semaphore_signal(barrier, inc=1, device_id={"tp": tp_peer(offset)}, device_id_type=MESH)
    for offset in range(1, SIDES):
        pl.semaphore_signal(barrier, inc=1, device_id={"rep": side_peer(offset)[1]}, device_id_type=MESH)
    for offset in range(1, DEPTH):
        pl.semaphore_signal(barrier, inc=1, device_id={"rep": z_peer(offset)[1]}, device_id_type=MESH)

    own_cols = pl.ds(pl.multiple_of(tp * width, width), width)
    own_rows = pl.ds(pl.multiple_of(tp * own, own), own)

    loads = [
        pltpu.make_async_copy(src, dst, load_sem.at[i])
        for i, (src, dst) in enumerate(
            [
                (tokens_ref, x_full.at[:, own_cols]),
                (bias_hbm, bias_ref),
                (counts_hbm, counts_ref),
                (lengths_hbm, lengths_ref),
                (deal_hbm, deal_ref),
                (attn_gain_hbm, attn_gain_ref),
                (ffn_gain_hbm, ffn_gain_ref),
                (w_query_ref, w_qkv.at[:, pl.ds(0, width)]),
                (w_key_ref, w_qkv.at[:, pl.ds(width, width)]),
                (w_value_ref, w_qkv.at[:, pl.ds(2 * width, width)]),
                (cache_k_ref, cache_k),
                (cache_v_ref, cache_v),
                (w_out_ref, w_out),
                (w_inner_ref, w_inner),
                (w_outer_ref, w_outer),
            ]
        )
    ]
    for load in loads:
        load.start()

    pl.semaphore_wait(barrier, (TP - 1) + (SIDES - 1) + (DEPTH - 1))

    loads[0].wait()
    gathers = []
    for offset in (2, 1, 3):
        copy = pltpu.make_async_remote_copy(
            src_ref=x_full.at[:, own_cols],
            dst_ref=x_full.at[:, own_cols],
            send_sem=ag_send.at[offset - 1],
            recv_sem=ag_recv.at[offset - 1],
            device_id={"tp": tp_peer(offset)},
            device_id_type=MESH,
        )
        copy.start()
        gathers.append(copy)

    for load in loads[1:7]:
        load.wait()

    key = iota((slots, keys), 1)
    query = iota((slots, keys), 0)
    for r in range(requests):
        length = lengths_ref[r]
        position = jnp.where(key < cached, key, length + key - cached)
        bucket = bucket_of(position - (length + query))
        rows = [jnp.zeros((slots, keys), F32) for _ in range(heads)]
        for b in range(BUCKETS):
            here = bucket == b
            rows = [jnp.where(here, bias_ref[h, b], rows[h]) for h in range(heads)]
        for h in range(heads):
            bias[r, pl.ds(h * slots, slots), :] = rows[h]

    q_row = iota((tokens, tokens), 0)
    k_col = iota((tokens, tokens), 1)
    q_side, q_z = q_row // DEPTH, q_row % DEPTH
    destination = (q_side // 2) * (2 * DEPTH) + q_z * 2 + q_side % 2
    count_of = jnp.where(k_col // slots == 0, counts_ref[0], counts_ref[requests - 1])
    live = (k_col % slots) < count_of
    order = jnp.where((deal_ref[...] == destination) & live, 1.0, 0.0)

    for copy in gathers:
        copy.wait_recv()

    stream = x_full[...].astype(F32)
    inverse = lax.rsqrt(jnp.mean(stream * stream, axis=1, keepdims=True) + EPSILON)
    normed = (stream * inverse * attn_gain_ref[...]).astype(BF16)
    for load in loads[7:10]:
        load.wait()
    qkv = dot(normed, w_qkv[...]).astype(BF16)

    loads[10].wait()
    loads[11].wait()
    lane_head = iota((slots, width), 1) // hdim
    key_row = iota((heads * slots, keys), 1)
    contexts = []
    for r in range(requests):
        rows = slice(r * slots, (r + 1) * slots)
        queries = qkv[rows, 0:width]
        all_keys = jnp.concatenate([cache_k[r], qkv[rows, width : 2 * width]], axis=0)
        all_values = jnp.concatenate([cache_v[r], qkv[rows, 2 * width :]], axis=0)
        stacked = jnp.concatenate(
            [jnp.where(lane_head == h, queries, jnp.zeros_like(queries)) for h in range(heads)], axis=0
        )
        scores = dot_t(stacked, all_keys) + bias[r]
        limit = jnp.where(key_row < cached, lengths_ref[r], cached + counts_ref[r])
        scores = jnp.where(key_row < limit, scores, -1e30)
        weights = jnp.exp(scores - jnp.max(scores, axis=1, keepdims=True))
        probs = (weights / jnp.sum(weights, axis=1, keepdims=True)).astype(BF16)
        spread = dot(probs, all_values)
        context = jnp.zeros((slots, width), F32)
        for h in range(heads):
            context = jnp.where(lane_head == h, spread[h * slots : (h + 1) * slots], context)
        contexts.append(context.astype(BF16))
    context = jnp.concatenate(contexts, axis=0)

    moved = dot(order.astype(BF16), context).astype(BF16)
    loads[12].wait()
    partial[...] = dot(moved, w_out[...])
    send_rows[...] = partial[...].astype(BF16)
    row_sends = []
    for offset in (2, 1, 3):
        peer = tp_peer(offset)
        copy = pltpu.make_async_remote_copy(
            src_ref=send_rows.at[pl.ds(pl.multiple_of(peer * own, own), own), :],
            dst_ref=recv_rows.at[offset - 1],
            send_sem=rs_send.at[offset - 1],
            recv_sem=rs_recv.at[offset - 1],
            device_id={"tp": peer},
            device_id_type=MESH,
        )
        copy.start()
        row_sends.append(copy)

    own_q = iota((own, tokens), 0) + tp * own
    own_k = iota((own, tokens), 1)
    own_side, own_z = own_q // DEPTH, own_q % DEPTH
    own_destination = (own_side // 2) * (2 * DEPTH) + own_z * 2 + own_side % 2
    own_count = jnp.where(own_k // slots == 0, counts_ref[0], counts_ref[requests - 1])
    own_order = one_hot((deal_ref[...] == own_destination) & ((own_k % slots) < own_count))
    mixed = dot(own_order, x_full[...]) + partial[own_rows, :]

    for copy in row_sends:
        copy.wait_recv()
    mixed = mixed + (recv_rows[0].astype(F32) + recv_rows[1].astype(F32) + recv_rows[2].astype(F32))
    inverse_ffn = lax.rsqrt(jnp.mean(mixed * mixed, axis=1, keepdims=True) + EPSILON)
    ffn_full[own_rows, :] = (mixed * inverse_ffn * ffn_gain_ref[...]).astype(BF16)
    ffn_gathers = []
    for offset in (2, 1, 3):
        copy = pltpu.make_async_remote_copy(
            src_ref=ffn_full.at[own_rows, :],
            dst_ref=ffn_full.at[own_rows, :],
            send_sem=ag2_send.at[offset - 1],
            recv_sem=ag2_recv.at[offset - 1],
            device_id={"tp": tp_peer(offset)},
            device_id_type=MESH,
        )
        copy.start()
        ffn_gathers.append(copy)
    loads[13].wait()
    loads[14].wait()
    for copy in ffn_gathers:
        copy.wait_recv()

    hidden = jnp.maximum(dot(ffn_full[...], w_inner[...]), 0.0).astype(BF16)
    partial[...] = dot(hidden, w_outer[...])
    partial[own_rows, :] = partial[own_rows, :] + mixed
    send_cols[...] = partial[...].astype(BF16)
    col_sends = []
    for offset in (2, 1, 3):
        peer = tp_peer(offset)
        copy = pltpu.make_async_remote_copy(
            src_ref=send_cols.at[:, pl.ds(pl.multiple_of(peer * width, width), width)],
            dst_ref=recv_cols.at[offset - 1],
            send_sem=rs2_send.at[offset - 1],
            recv_sem=rs2_recv.at[offset - 1],
            device_id={"tp": peer},
            device_id_type=MESH,
        )
        copy.start()
        col_sends.append(copy)
    to_row = iota((2 * tokens, 2 * tokens), 0)
    to_col = iota((2 * tokens, 2 * tokens), 1)
    gather_z = one_hot(
        to_col
        == ((to_row // SIDES) % 2) * tokens + (to_row % SIDES) * DEPTH + to_row // (2 * SIDES)
    )
    final = partial[:, own_cols]
    for copy in col_sends:
        copy.wait_recv()
    final = final + (recv_cols[0].astype(F32) + recv_cols[1].astype(F32) + recv_cols[2].astype(F32))
    side_send[...] = final.astype(BF16).reshape(SIDES, DEPTH, width)

    side_sends = []
    for offset in range(1, SIDES):
        other, peer = side_peer(offset)
        copy = pltpu.make_async_remote_copy(
            src_ref=side_send.at[other],
            dst_ref=side_recv.at[side],
            send_sem=side_send_sem.at[offset - 1],
            recv_sem=side_recv_sem.at[offset - 1],
            device_id={"rep": peer},
            device_id_type=MESH,
        )
        copy.start()
        side_sends.append(copy)
    side_recv[side] = side_send[side]
    d_row = iota((tokens, 2 * tokens), 0)
    d_col = iota((tokens, 2 * tokens), 1)
    d_from = ((d_row // 2) % DEPTH) * (2 * SIDES) + (d_row // (2 * DEPTH)) * 2 + d_row % 2
    left = one_hot(d_col == d_from)
    right = one_hot(d_col == d_from + SIDES)
    for copy in side_sends:
        copy.wait_recv()

    arrived = side_recv[...].reshape(tokens, width)
    halves = jnp.concatenate([arrived[:, : width // 2], arrived[:, width // 2 :]], axis=0)
    z_send[...] = dot(gather_z, halves).astype(BF16).reshape(DEPTH, 2 * SIDES, width // 2)
    z_sends = []
    for offset in range(1, DEPTH):
        other, peer = z_peer(offset)
        copy = pltpu.make_async_remote_copy(
            src_ref=z_send.at[other],
            dst_ref=z_recv.at[z_at],
            send_sem=z_send_sem.at[offset - 1],
            recv_sem=z_recv_sem.at[offset - 1],
            device_id={"rep": peer},
            device_id_type=MESH,
        )
        copy.start()
        z_sends.append(copy)
    z_recv[z_at] = z_send[z_at]
    for copy in gathers + row_sends + ffn_gathers + col_sends + side_sends:
        copy.wait_send()
    for copy in z_sends:
        copy.wait_recv()
    landed = z_recv[...].reshape(2 * tokens, width // 2)
    out_ref[:, : width // 2] = dot(left, landed).astype(BF16)
    out_ref[:, width // 2 :] = dot(right, landed).astype(BF16)
    for copy in z_sends:
        copy.wait_send()


def on_device(
    tokens,
    attn_gain,
    ffn_gain,
    w_query,
    w_key,
    w_value,
    w_out,
    w_inner,
    w_outer,
    bias_table,
    cache_keys,
    cache_values,
    new_counts,
    cached_lengths,
    deal,
):
    rows, width = tokens.shape
    model = w_query.shape[0]
    ff = w_inner.shape[1]
    requests, cached, _ = cache_keys.shape
    slots = rows // requests
    heads = bias_table.shape[1]
    own = rows // TP
    hbm = pl.BlockSpec(memory_space=pltpu.HBM)
    vmem = pl.BlockSpec(memory_space=pltpu.VMEM)
    dma = pltpu.SemaphoreType.DMA
    return pl.pallas_call(
        kernel,
        out_shape=jax.ShapeDtypeStruct((rows, width), BF16),
        in_specs=[hbm] * 15,
        out_specs=vmem,
        scratch_shapes=[
            pltpu.VMEM((1, model), F32),
            pltpu.VMEM((1, model), F32),
            pltpu.SMEM((heads, BUCKETS), F32),
            pltpu.SMEM((requests,), jnp.int32),
            pltpu.SMEM((requests,), jnp.int32),
            pltpu.VMEM((1, rows), jnp.int32),
            pltpu.VMEM((rows, model), BF16),
            pltpu.VMEM((model, 3 * width), BF16),
            pltpu.VMEM((width, model), BF16),
            pltpu.VMEM((model, ff), BF16),
            pltpu.VMEM((ff, model), BF16),
            pltpu.VMEM((requests, cached, width), BF16),
            pltpu.VMEM((requests, cached, width), BF16),
            pltpu.VMEM((requests, heads * slots, cached + slots), F32),
            pltpu.VMEM((rows, model), F32),
            pltpu.VMEM((rows, model), BF16),
            pltpu.VMEM((TP - 1, own, model), BF16),
            pltpu.VMEM((rows, model), BF16),
            pltpu.VMEM((rows, model), BF16),
            pltpu.VMEM((TP - 1, rows, width), BF16),
            pltpu.VMEM((SIDES, DEPTH, width), BF16),
            pltpu.VMEM((SIDES, DEPTH, width), BF16),
            pltpu.VMEM((DEPTH, 2 * SIDES, width // 2), BF16),
            pltpu.VMEM((DEPTH, 2 * SIDES, width // 2), BF16),
            dma((15,)),
            dma((TP - 1,)),
            dma((TP - 1,)),
            dma((TP - 1,)),
            dma((TP - 1,)),
            dma((TP - 1,)),
            dma((TP - 1,)),
            dma((TP - 1,)),
            dma((TP - 1,)),
            dma((SIDES - 1,)),
            dma((SIDES - 1,)),
            dma((DEPTH - 1,)),
            dma((DEPTH - 1,)),
        ],
        compiler_params=pltpu.CompilerParams(
            collective_id=0, has_side_effects=True, vmem_limit_bytes=60 * 1024 * 1024
        ),
    )(
        tokens,
        attn_gain.reshape(1, model),
        ffn_gain.reshape(1, model),
        w_query,
        w_key,
        w_value,
        w_out,
        w_inner,
        w_outer,
        bias_table.T,
        cache_keys,
        cache_values,
        new_counts.reshape(requests),
        cached_lengths.reshape(requests),
        deal,
    )


def solution(mesh):
    in_specs = (
        P("rep", "tp"),
        P(),
        P(),
        P(None, "tp"),
        P(None, "tp"),
        P(None, "tp"),
        P("tp", None),
        P(None, "tp"),
        P("tp", None),
        P(None, "tp"),
        P("rep", None, "tp"),
        P("rep", None, "tp"),
        P(None, "rep"),
        P(None, "rep"),
        P("rep", None),
    )
    out_specs = P("rep", "tp")
    return jax.shard_map(
        on_device, mesh=mesh, in_specs=in_specs, out_specs=out_specs, check_vma=False
    )
```

```python
import jax
import jax.numpy as jnp
from jax import lax
from jax.experimental import pallas as pl
from jax.experimental.pallas import tpu as pltpu
from jax.sharding import PartitionSpec as P

EPSILON = 1e-06
THRESHOLDS = (12, 16, 23, 32, 46, 64, 91)
BUCKETS = 32
TP = 4
REPLICAS = 128
SIDES = 8
DEPTH = 16
LANES_OF_ROW = 8
FAR_FIRST = sorted(range(1, 32), key=lambda slot: -min(2 * slot % DEPTH, -2 * slot % DEPTH))
NEAR = (1, 2, 14, 15)
MESH = pl.DeviceIdType.MESH
BF16 = jnp.bfloat16
F32 = jnp.float32


def iota(shape, dim):
    return lax.broadcasted_iota(jnp.int32, shape, dim)


def dot(a, b):
    return jnp.dot(a, b, preferred_element_type=F32)


def dot_t(a, b):
    return lax.dot_general(a, b, (((1,), (1,)), ((), ())), preferred_element_type=F32)


def bucket_of(relative):
    distance = jnp.abs(relative)
    larger = 8 + sum(((distance >= threshold).astype(jnp.int32) for threshold in THRESHOLDS))
    near = jnp.where(distance < 8, distance, larger)
    return near + 16 * (relative > 0).astype(jnp.int32)


def one_hot(condition):
    return jnp.where(condition, 1.0, 0.0).astype(BF16)


def kernel(
    tokens_ref,
    attn_gain_hbm,
    ffn_gain_hbm,
    w_query_ref,
    w_key_ref,
    w_value_ref,
    w_out_ref,
    w_inner_ref,
    w_outer_ref,
    bias_hbm,
    cache_k_ref,
    cache_v_ref,
    counts_hbm,
    lengths_hbm,
    deal_hbm,
    out_ref,
    attn_gain_ref,
    ffn_gain_ref,
    bias_ref,
    counts_ref,
    lengths_ref,
    deal_ref,
    x_full,
    w_qkv,
    w_out,
    w_inner,
    w_outer,
    cache_k,
    cache_v,
    bias,
    partial,
    send_rows,
    recv_rows,
    ffn_full,
    send_cols,
    recv_cols,
    slab,
    deal_send,
    deal_recv,
    load_sem,
    ag_send,
    ag_recv,
    rs_send,
    rs_recv,
    ag2_send,
    ag2_recv,
    rs2_send,
    rs2_recv,
    deal_send_sem,
    deal_recv_sem,
    relay_two,
    relay_four,
    relay_side,
):
    rep = lax.axis_index("rep")
    tp = lax.axis_index("tp")
    tokens, width = tokens_ref.shape
    model = w_qkv.shape[0]
    requests, cached, _ = cache_k_ref.shape
    slots = tokens // requests
    heads = bias_ref.shape[0]
    hdim = width // heads
    keys = cached + slots
    own = tokens // TP
    x_at, z_at, core = rep // (2 * DEPTH), (rep // 2) % DEPTH, rep % 2
    side = x_at * 2 + core

    def tp_peer(offset):
        return (tp + offset) % TP

    def side_peer(offset):
        other = (side + offset) % SIDES
        return (other // 2) * (2 * DEPTH) + z_at * 2 + other % 2

    def z_peer(offset):
        return x_at * (2 * DEPTH) + ((z_at + offset) % DEPTH) * 2 + core

    def greet(semaphore, peer):
        pl.semaphore_signal(semaphore, inc=1, device_id={"rep": peer}, device_id_type=MESH)

    barrier = pltpu.get_barrier_semaphore()
    for offset in range(1, TP):
        pl.semaphore_signal(barrier, inc=1, device_id={"tp": tp_peer(offset)}, device_id_type=MESH)
    for offset in range(1, SIDES):
        greet(barrier, side_peer(offset))
    for offset in NEAR:
        greet(barrier, z_peer(offset))

    own_cols = pl.ds(pl.multiple_of(tp * width, width), width)
    own_rows = pl.ds(pl.multiple_of(tp * own, own), own)

    loads = [
        pltpu.make_async_copy(src, dst, load_sem.at[i])
        for i, (src, dst) in enumerate(
            [
                (tokens_ref, x_full.at[:, own_cols]),
                (bias_hbm, bias_ref),
                (counts_hbm, counts_ref),
                (lengths_hbm, lengths_ref),
                (deal_hbm, deal_ref),
                (attn_gain_hbm, attn_gain_ref),
                (ffn_gain_hbm, ffn_gain_ref),
                (w_query_ref, w_qkv.at[:, pl.ds(0, width)]),
                (w_key_ref, w_qkv.at[:, pl.ds(width, width)]),
                (w_value_ref, w_qkv.at[:, pl.ds(2 * width, width)]),
                (cache_k_ref, cache_k),
                (cache_v_ref, cache_v),
                (w_out_ref, w_out),
                (w_inner_ref, w_inner),
                (w_outer_ref, w_outer),
            ]
        )
    ]
    for load in loads:
        load.start()

    pl.semaphore_wait(barrier, (TP - 1) + (SIDES - 1) + len(NEAR))
    for offset in (2, DEPTH - 2):
        greet(relay_two, z_peer(offset))

    loads[0].wait()
    gathers = []
    for offset in (2, 1, 3):
        copy = pltpu.make_async_remote_copy(
            src_ref=x_full.at[:, own_cols],
            dst_ref=x_full.at[:, own_cols],
            send_sem=ag_send.at[offset - 1],
            recv_sem=ag_recv.at[offset - 1],
            device_id={"tp": tp_peer(offset)},
            device_id_type=MESH,
        )
        copy.start()
        gathers.append(copy)

    for load in loads[1:7]:
        load.wait()

    key = iota((slots, keys), 1)
    query = iota((slots, keys), 0)
    for r in range(requests):
        length = lengths_ref[r]
        position = jnp.where(key < cached, key, length + key - cached)
        bucket = bucket_of(position - (length + query))
        rows = [jnp.zeros((slots, keys), F32) for _ in range(heads)]
        for b in range(BUCKETS):
            here = bucket == b
            rows = [jnp.where(here, bias_ref[h, b], rows[h]) for h in range(heads)]
        for h in range(heads):
            bias[r, pl.ds(h * slots, slots), :] = rows[h]

    q_row = iota((tokens, tokens), 0)
    k_col = iota((tokens, tokens), 1)
    destination = (rep + q_row // own + TP * (q_row % own)) % REPLICAS
    count_of = jnp.where(k_col // slots == 0, counts_ref[0], counts_ref[requests - 1])
    live = (k_col % slots) < count_of
    order = jnp.where((deal_ref[...] == destination) & live, 1.0, 0.0)

    pl.semaphore_wait(relay_two, 2)
    for offset in (4, DEPTH - 4):
        greet(relay_four, z_peer(offset))

    for copy in gathers:
        copy.wait_recv()

    stream = x_full[...].astype(F32)
    inverse = lax.rsqrt(jnp.mean(stream * stream, axis=1, keepdims=True) + EPSILON)
    normed = (stream * inverse * attn_gain_ref[...]).astype(BF16)
    for load in loads[7:10]:
        load.wait()
    qkv = dot(normed, w_qkv[...]).astype(BF16)

    loads[10].wait()
    loads[11].wait()
    lane_head = iota((slots, width), 1) // hdim
    key_row = iota((heads * slots, keys), 1)
    contexts = []
    for r in range(requests):
        rows = slice(r * slots, (r + 1) * slots)
        queries = qkv[rows, 0:width]
        all_keys = jnp.concatenate([cache_k[r], qkv[rows, width : 2 * width]], axis=0)
        all_values = jnp.concatenate([cache_v[r], qkv[rows, 2 * width :]], axis=0)
        stacked = jnp.concatenate(
            [jnp.where(lane_head == h, queries, jnp.zeros_like(queries)) for h in range(heads)], axis=0
        )
        scores = dot_t(stacked, all_keys) + bias[r]
        limit = jnp.where(key_row < cached, lengths_ref[r], cached + counts_ref[r])
        scores = jnp.where(key_row < limit, scores, -1e30)
        weights = jnp.exp(scores - jnp.max(scores, axis=1, keepdims=True))
        probs = (weights / jnp.sum(weights, axis=1, keepdims=True)).astype(BF16)
        spread = dot(probs, all_values)
        context = jnp.zeros((slots, width), F32)
        for h in range(heads):
            context = jnp.where(lane_head == h, spread[h * slots : (h + 1) * slots], context)
        contexts.append(context.astype(BF16))
    context = jnp.concatenate(contexts, axis=0)

    moved = dot(order.astype(BF16), context).astype(BF16)
    loads[12].wait()
    partial[...] = dot(moved, w_out[...])
    send_rows[...] = partial[...].astype(BF16)
    row_sends = []
    for offset in (2, 1, 3):
        peer = tp_peer(offset)
        copy = pltpu.make_async_remote_copy(
            src_ref=send_rows.at[pl.ds(pl.multiple_of(peer * own, own), own), :],
            dst_ref=recv_rows.at[offset - 1],
            send_sem=rs_send.at[offset - 1],
            recv_sem=rs_recv.at[offset - 1],
            device_id={"tp": peer},
            device_id_type=MESH,
        )
        copy.start()
        row_sends.append(copy)

    pl.semaphore_wait(relay_four, 2)
    for offset in range(1, SIDES):
        greet(relay_side, side_peer(offset))

    own_q = iota((own, tokens), 0)
    own_k = iota((own, tokens), 1)
    own_destination = (rep + tp + TP * own_q) % REPLICAS
    own_count = jnp.where(own_k // slots == 0, counts_ref[0], counts_ref[requests - 1])
    own_order = one_hot((deal_ref[...] == own_destination) & ((own_k % slots) < own_count))
    mixed = dot(own_order, x_full[...]) + partial[own_rows, :]

    for copy in row_sends:
        copy.wait_recv()
    mixed = mixed + (recv_rows[0].astype(F32) + recv_rows[1].astype(F32) + recv_rows[2].astype(F32))
    for c in range(LANES_OF_ROW):
        slab[pl.ds(c, own, stride=LANES_OF_ROW), :] = mixed[:, c * 128 : (c + 1) * 128]
    deal_send[...] = slab[...].reshape(own, LANES_OF_ROW, 128).astype(BF16)

    pl.semaphore_wait(relay_side, SIDES - 1)

    def deal(slot):
        return pltpu.make_async_remote_copy(
            src_ref=deal_send.at[slot],
            dst_ref=deal_recv.at[slot],
            send_sem=deal_send_sem.at[slot],
            recv_sem=deal_recv_sem.at[slot],
            device_id={"rep": (rep + tp + TP * slot) % REPLICAS},
            device_id_type=MESH,
        )

    for slot in FAR_FIRST:
        deal(slot).start()

    stays = pltpu.make_async_copy(deal_send.at[0], deal_recv.at[0], deal_recv_sem.at[0])

    @pl.when(tp == 0)
    def _():
        stays.start()

    @pl.when(tp != 0)
    def _():
        deal(0).start()

    for slot in range(1, own):
        deal(slot).wait_recv()
    stays.wait()
    slab[...] = deal_recv[...].astype(F32).reshape(own * LANES_OF_ROW, 128)
    mixed = jnp.concatenate(
        [slab[pl.ds(c, own, stride=LANES_OF_ROW), :] for c in range(LANES_OF_ROW)], axis=1
    )
    inverse_ffn = lax.rsqrt(jnp.mean(mixed * mixed, axis=1, keepdims=True) + EPSILON)
    ffn_full[own_rows, :] = (mixed * inverse_ffn * ffn_gain_ref[...]).astype(BF16)
    ffn_gathers = []
    for offset in (2, 1, 3):
        copy = pltpu.make_async_remote_copy(
            src_ref=ffn_full.at[own_rows, :],
            dst_ref=ffn_full.at[own_rows, :],
            send_sem=ag2_send.at[offset - 1],
            recv_sem=ag2_recv.at[offset - 1],
            device_id={"tp": tp_peer(offset)},
            device_id_type=MESH,
        )
        copy.start()
        ffn_gathers.append(copy)
    loads[13].wait()
    loads[14].wait()
    for copy in ffn_gathers:
        copy.wait_recv()

    hidden = jnp.maximum(dot(ffn_full[...], w_inner[...]), 0.0).astype(BF16)
    partial[...] = dot(hidden, w_outer[...])
    partial[own_rows, :] = partial[own_rows, :] + mixed
    send_cols[...] = partial[...].astype(BF16)
    col_sends = []
    for offset in (2, 1, 3):
        peer = tp_peer(offset)
        copy = pltpu.make_async_remote_copy(
            src_ref=send_cols.at[:, pl.ds(pl.multiple_of(peer * width, width), width)],
            dst_ref=recv_cols.at[offset - 1],
            send_sem=rs2_send.at[offset - 1],
            recv_sem=rs2_recv.at[offset - 1],
            device_id={"tp": peer},
            device_id_type=MESH,
        )
        copy.start()
        col_sends.append(copy)
    from_row = iota((tokens, tokens), 1)
    source = (rep + REPLICAS * 2 - from_row // own - TP * (from_row % own)) % REPLICAS
    restore = one_hot(iota((tokens, tokens), 0) == source)
    final = partial[:, own_cols]
    for copy in col_sends:
        copy.wait_recv()
    final = final + (recv_cols[0].astype(F32) + recv_cols[1].astype(F32) + recv_cols[2].astype(F32))
    out_ref[...] = dot(restore, final.astype(BF16)).astype(BF16)
    for copy in gathers + row_sends + ffn_gathers + col_sends:
        copy.wait_send()
    for slot in range(1, own):
        deal(slot).wait_send()

    @pl.when(tp != 0)
    def _():
        deal(0).wait_send()


def on_device(
    tokens,
    attn_gain,
    ffn_gain,
    w_query,
    w_key,
    w_value,
    w_out,
    w_inner,
    w_outer,
    bias_table,
    cache_keys,
    cache_values,
    new_counts,
    cached_lengths,
    deal,
):
    rows, width = tokens.shape
    model = w_query.shape[0]
    ff = w_inner.shape[1]
    requests, cached, _ = cache_keys.shape
    slots = rows // requests
    heads = bias_table.shape[1]
    own = rows // TP
    hbm = pl.BlockSpec(memory_space=pltpu.HBM)
    vmem = pl.BlockSpec(memory_space=pltpu.VMEM)
    dma = pltpu.SemaphoreType.DMA
    return pl.pallas_call(
        kernel,
        out_shape=jax.ShapeDtypeStruct((rows, width), BF16),
        in_specs=[hbm] * 15,
        out_specs=vmem,
        scratch_shapes=[
            pltpu.VMEM((1, model), F32),
            pltpu.VMEM((1, model), F32),
            pltpu.SMEM((heads, BUCKETS), F32),
            pltpu.SMEM((requests,), jnp.int32),
            pltpu.SMEM((requests,), jnp.int32),
            pltpu.VMEM((1, rows), jnp.int32),
            pltpu.VMEM((rows, model), BF16),
            pltpu.VMEM((model, 3 * width), BF16),
            pltpu.VMEM((width, model), BF16),
            pltpu.VMEM((model, ff), BF16),
            pltpu.VMEM((ff, model), BF16),
            pltpu.VMEM((requests, cached, width), BF16),
            pltpu.VMEM((requests, cached, width), BF16),
            pltpu.VMEM((requests, heads * slots, cached + slots), F32),
            pltpu.VMEM((rows, model), F32),
            pltpu.VMEM((rows, model), BF16),
            pltpu.VMEM((TP - 1, own, model), BF16),
            pltpu.VMEM((rows, model), BF16),
            pltpu.VMEM((rows, model), BF16),
            pltpu.VMEM((TP - 1, rows, width), BF16),
            pltpu.VMEM((own * LANES_OF_ROW, 128), F32),
            pltpu.VMEM((own, LANES_OF_ROW, 128), BF16),
            pltpu.VMEM((own, LANES_OF_ROW, 128), BF16),
            dma((15,)),
            dma((TP - 1,)),
            dma((TP - 1,)),
            dma((TP - 1,)),
            dma((TP - 1,)),
            dma((TP - 1,)),
            dma((TP - 1,)),
            dma((TP - 1,)),
            dma((TP - 1,)),
            dma((own,)),
            dma((own,)),
            pltpu.SemaphoreType.REGULAR,
            pltpu.SemaphoreType.REGULAR,
            pltpu.SemaphoreType.REGULAR,
        ],
        compiler_params=pltpu.CompilerParams(
            collective_id=0, has_side_effects=True, vmem_limit_bytes=60 * 1024 * 1024
        ),
    )(
        tokens,
        attn_gain.reshape(1, model),
        ffn_gain.reshape(1, model),
        w_query,
        w_key,
        w_value,
        w_out,
        w_inner,
        w_outer,
        bias_table.T,
        cache_keys,
        cache_values,
        new_counts.reshape(requests),
        cached_lengths.reshape(requests),
        deal,
    )


def solution(mesh):
    in_specs = (
        P("rep", "tp"),
        P(),
        P(),
        P(None, "tp"),
        P(None, "tp"),
        P(None, "tp"),
        P("tp", None),
        P(None, "tp"),
        P("tp", None),
        P(None, "tp"),
        P("rep", None, "tp"),
        P("rep", None, "tp"),
        P(None, "rep"),
        P(None, "rep"),
        P("rep", None),
    )
    out_specs = P("rep", "tp")
    return jax.shard_map(
        on_device, mesh=mesh, in_specs=in_specs, out_specs=out_specs, check_vma=False
    )
```

```python
import jax
import jax.numpy as jnp
from jax import lax
from jax.experimental import pallas as pl
from jax.experimental.pallas import tpu as pltpu
from jax.sharding import PartitionSpec as P

EPSILON = 1e-06
THRESHOLDS = (12, 16, 23, 32, 46, 64, 91)
BUCKETS = 32
TP = 4
REPLICAS = 128
SIDES = 8
DEPTH = 16
LANES_OF_ROW = 8
HALF = 16
NEAR = (1, 2, 14, 15)
MESH = pl.DeviceIdType.MESH
BF16 = jnp.bfloat16
F32 = jnp.float32


def iota(shape, dim):
    return lax.broadcasted_iota(jnp.int32, shape, dim)


def dot(a, b):
    return jnp.dot(a, b, preferred_element_type=F32)


def dot_t(a, b):
    return lax.dot_general(a, b, (((1,), (1,)), ((), ())), preferred_element_type=F32)


def bucket_of(relative):
    distance = jnp.abs(relative)
    larger = 8 + sum(((distance >= threshold).astype(jnp.int32) for threshold in THRESHOLDS))
    near = jnp.where(distance < 8, distance, larger)
    return near + 16 * (relative > 0).astype(jnp.int32)


def step_of(slot):
    return ((slot % HALF) // 4) * 8 + (slot % 4 + 6 + 4 * (slot // HALF)) % 8


STAYS = 2


def far_first(slots):
    return sorted(slots, key=lambda slot: -min(2 * step_of(slot) % DEPTH, -2 * step_of(slot) % DEPTH))


def one_hot(condition):
    return jnp.where(condition, 1.0, 0.0).astype(BF16)


def kernel(
    tokens_ref,
    attn_gain_hbm,
    ffn_gain_hbm,
    w_query_ref,
    w_key_ref,
    w_value_ref,
    w_out_ref,
    w_inner_ref,
    w_outer_ref,
    bias_hbm,
    cache_k_ref,
    cache_v_ref,
    counts_hbm,
    lengths_hbm,
    deal_hbm,
    out_ref,
    attn_gain_ref,
    ffn_gain_ref,
    bias_ref,
    counts_ref,
    lengths_ref,
    deal_ref,
    x_full,
    w_qkv,
    w_out,
    w_inner,
    w_outer,
    cache_k,
    cache_v,
    bias,
    partial,
    send_rows,
    recv_rows,
    ffn_full,
    send_cols,
    recv_cols,
    mixed_ref,
    slab,
    deal_send,
    deal_recv,
    load_sem,
    ag_send,
    ag_recv,
    rs_send,
    rs_recv,
    ag2_send,
    ag2_recv,
    rs2_send,
    rs2_recv,
    deal_send_sem,
    deal_recv_sem,
    relay_two,
    relay_four,
    relay_side,
):
    rep = lax.axis_index("rep")
    tp = lax.axis_index("tp")
    tokens, width = tokens_ref.shape
    model = w_qkv.shape[0]
    requests, cached, _ = cache_k_ref.shape
    slots = tokens // requests
    heads = bias_ref.shape[0]
    hdim = width // heads
    keys = cached + slots
    own = tokens // TP
    x_at, z_at, core = rep // (2 * DEPTH), (rep // 2) % DEPTH, rep % 2
    side = x_at * 2 + core

    def tp_peer(offset):
        return (tp + offset) % TP

    def side_peer(offset):
        other = (side + offset) % SIDES
        return (other // 2) * (2 * DEPTH) + z_at * 2 + other % 2

    def z_peer(offset):
        return x_at * (2 * DEPTH) + ((z_at + offset) % DEPTH) * 2 + core

    def greet(semaphore, peer):
        pl.semaphore_signal(semaphore, inc=1, device_id={"rep": peer}, device_id_type=MESH)

    barrier = pltpu.get_barrier_semaphore()
    for offset in range(1, TP):
        pl.semaphore_signal(barrier, inc=1, device_id={"tp": tp_peer(offset)}, device_id_type=MESH)
    for offset in range(1, SIDES):
        greet(barrier, side_peer(offset))
    for offset in NEAR:
        greet(barrier, z_peer(offset))

    own_cols = pl.ds(pl.multiple_of(tp * width, width), width)

    def group_rows(half, group):
        return pl.ds(pl.multiple_of((half * TP + group) * HALF, HALF), HALF)


    loads = [
        pltpu.make_async_copy(src, dst, load_sem.at[i])
        for i, (src, dst) in enumerate(
            [
                (tokens_ref, x_full.at[:, own_cols]),
                (bias_hbm, bias_ref),
                (counts_hbm, counts_ref),
                (lengths_hbm, lengths_ref),
                (deal_hbm, deal_ref),
                (attn_gain_hbm, attn_gain_ref),
                (ffn_gain_hbm, ffn_gain_ref),
                (w_query_ref, w_qkv.at[:, pl.ds(0, width)]),
                (w_key_ref, w_qkv.at[:, pl.ds(width, width)]),
                (w_value_ref, w_qkv.at[:, pl.ds(2 * width, width)]),
                (cache_k_ref, cache_k),
                (cache_v_ref, cache_v),
                (w_out_ref, w_out),
                (w_inner_ref, w_inner),
                (w_outer_ref, w_outer),
            ]
        )
    ]
    for load in loads:
        load.start()

    pl.semaphore_wait(barrier, (TP - 1) + (SIDES - 1) + len(NEAR))
    for offset in (2, DEPTH - 2):
        greet(relay_two, z_peer(offset))

    loads[0].wait()
    gathers = []
    for offset in (2, 1, 3):
        copy = pltpu.make_async_remote_copy(
            src_ref=x_full.at[:, own_cols],
            dst_ref=x_full.at[:, own_cols],
            send_sem=ag_send.at[offset - 1],
            recv_sem=ag_recv.at[offset - 1],
            device_id={"tp": tp_peer(offset)},
            device_id_type=MESH,
        )
        copy.start()
        gathers.append(copy)

    for load in loads[1:7]:
        load.wait()

    def squares_of(chunk):
        cols = pl.ds(pl.multiple_of(chunk * width, width), width)
        stream = x_full[:, cols].astype(F32)
        return jnp.sum(stream * stream, axis=1, keepdims=True)

    squares = squares_of(tp)

    key = iota((slots, keys), 1)
    query = iota((slots, keys), 0)
    for r in range(requests):
        length = lengths_ref[r]
        position = jnp.where(key < cached, key, length + key - cached)
        bucket = bucket_of(position - (length + query))
        rows = [jnp.zeros((slots, keys), F32) for _ in range(heads)]
        for b in range(BUCKETS):
            here = bucket == b
            rows = [jnp.where(here, bias_ref[h, b], rows[h]) for h in range(heads)]
        for h in range(heads):
            bias[r, pl.ds(h * slots, slots), :] = rows[h]

    q_row = iota((tokens, tokens), 0)
    k_col = iota((tokens, tokens), 1)
    q_group = (q_row // HALF) % TP
    q_step = step_of(q_row // (TP * HALF) * HALF + q_row % HALF)
    destination = (rep + q_group + TP * q_step) % REPLICAS
    count_of = jnp.where(k_col // slots == 0, counts_ref[0], counts_ref[requests - 1])
    live = (k_col % slots) < count_of
    order = jnp.where((deal_ref[...] == destination) & live, 1.0, 0.0)

    pl.semaphore_wait(relay_two, 2)
    for offset in (4, DEPTH - 4):
        greet(relay_four, z_peer(offset))

    for load in loads[7:10]:
        load.wait()
    for copy, offset in ((gathers[1], 1), (gathers[2], 3), (gathers[0], 2)):
        copy.wait_recv()
        squares += squares_of((tp + TP - offset) % TP)
    inverse = lax.rsqrt(squares / model + EPSILON)
    for c in range(TP):
        cols = slice(c * width, (c + 1) * width)
        send_rows[:, cols] = (x_full[:, cols].astype(F32) * inverse * attn_gain_ref[:, cols]).astype(BF16)
    qkv = dot(send_rows[...], w_qkv[...]).astype(BF16)

    loads[10].wait()
    loads[11].wait()
    lane_head = iota((slots, width), 1) // hdim
    key_row = iota((heads * slots, keys), 1)
    contexts = []
    for r in range(requests):
        rows = slice(r * slots, (r + 1) * slots)
        queries = qkv[rows, 0:width]
        all_keys = jnp.concatenate([cache_k[r], qkv[rows, width : 2 * width]], axis=0)
        all_values = jnp.concatenate([cache_v[r], qkv[rows, 2 * width :]], axis=0)
        stacked = jnp.concatenate(
            [jnp.where(lane_head == h, queries, jnp.zeros_like(queries)) for h in range(heads)], axis=0
        )
        scores = dot_t(stacked, all_keys) + bias[r]
        limit = jnp.where(key_row < cached, lengths_ref[r], cached + counts_ref[r])
        scores = jnp.where(key_row < limit, scores, -1e30)
        weights = jnp.exp(scores - jnp.max(scores, axis=1, keepdims=True))
        probs = (weights / jnp.sum(weights, axis=1, keepdims=True)).astype(BF16)
        spread = dot(probs, all_values)
        context = jnp.zeros((slots, width), F32)
        for h in range(heads):
            context = jnp.where(lane_head == h, spread[h * slots : (h + 1) * slots], context)
        contexts.append(context.astype(BF16))
    context = jnp.concatenate(contexts, axis=0)

    moved = dot(order.astype(BF16), context).astype(BF16)
    loads[12].wait()
    partial[...] = dot(moved, w_out[...])
    send_rows[...] = partial[...].astype(BF16)
    row_sends = [[], []]
    for half in (1, 0):
        for offset in (2, 1, 3):
            peer = tp_peer(offset)
            copy = pltpu.make_async_remote_copy(
                src_ref=send_rows.at[group_rows(half, peer), :],
                dst_ref=recv_rows.at[half, offset - 1],
                send_sem=rs_send.at[half, offset - 1],
                recv_sem=rs_recv.at[half, offset - 1],
                device_id={"tp": peer},
                device_id_type=MESH,
            )
            copy.start()
            row_sends[half].append(copy)

    pl.semaphore_wait(relay_four, 2)
    for offset in range(1, SIDES):
        greet(relay_side, side_peer(offset))

    own_q = iota((own, tokens), 0)
    own_k = iota((own, tokens), 1)
    own_destination = (rep + tp + TP * step_of(own_q)) % REPLICAS
    own_count = jnp.where(own_k // slots == 0, counts_ref[0], counts_ref[requests - 1])
    own_order = one_hot((deal_ref[...] == own_destination) & ((own_k % slots) < own_count))
    mixed_ref[...] = dot(own_order, x_full[...])

    def deal(slot):
        return pltpu.make_async_remote_copy(
            src_ref=deal_send.at[slot],
            dst_ref=deal_recv.at[slot],
            send_sem=deal_send_sem.at[slot],
            recv_sem=deal_recv_sem.at[slot],
            device_id={"rep": (rep + tp + TP * step_of(slot)) % REPLICAS},
            device_id_type=MESH,
        )

    stays = pltpu.make_async_copy(deal_send.at[STAYS], deal_recv.at[STAYS], deal_recv_sem.at[STAYS])
    lines = HALF * LANES_OF_ROW
    for half in (1, 0):
        for copy in row_sends[half]:
            copy.wait_recv()
        rows = slice(half * HALF, (half + 1) * HALF)
        arrived = [recv_rows[half, i].astype(F32) for i in range(TP - 1)]
        mixed = mixed_ref[rows, :] + partial[group_rows(half, tp), :] + (arrived[0] + arrived[1] + arrived[2])
        for c in range(LANES_OF_ROW):
            slab[pl.ds(half * lines + c, HALF, stride=LANES_OF_ROW), :] = mixed[:, c * 128 : (c + 1) * 128]
        deal_send[rows] = (
            slab[half * lines : (half + 1) * lines, :].reshape(HALF, LANES_OF_ROW, 128).astype(BF16)
        )
        if half == 1:
            pl.semaphore_wait(relay_side, SIDES - 1)
        for slot in far_first(range(half * HALF, (half + 1) * HALF)):
            if slot != STAYS:
                deal(slot).start()

    @pl.when(tp == 0)
    def _():
        stays.start()

    @pl.when(tp != 0)
    def _():
        deal(STAYS).start()

    ffn_gathers = [[], []]
    for half in (0, 1):
        rows = slice(half * HALF, (half + 1) * HALF)
        for slot in range(half * HALF, (half + 1) * HALF):
            if slot == STAYS:
                stays.wait()
            else:
                deal(slot).wait_recv()
        slab[half * lines : (half + 1) * lines, :] = deal_recv[rows].astype(F32).reshape(lines, 128)
        mixed = jnp.concatenate(
            [
                slab[pl.ds(half * lines + c, HALF, stride=LANES_OF_ROW), :]
                for c in range(LANES_OF_ROW)
            ],
            axis=1,
        )
        mixed_ref[rows, :] = mixed
        inverse_ffn = lax.rsqrt(jnp.mean(mixed * mixed, axis=1, keepdims=True) + EPSILON)
        ffn_full[group_rows(half, tp), :] = (mixed * inverse_ffn * ffn_gain_ref[...]).astype(BF16)
        for offset in (2, 1, 3):
            copy = pltpu.make_async_remote_copy(
                src_ref=ffn_full.at[group_rows(half, tp), :],
                dst_ref=ffn_full.at[group_rows(half, tp), :],
                send_sem=ag2_send.at[half, offset - 1],
                recv_sem=ag2_recv.at[half, offset - 1],
                device_id={"tp": tp_peer(offset)},
                device_id_type=MESH,
            )
            copy.start()
            ffn_gathers[half].append(copy)

    loads[13].wait()
    loads[14].wait()
    col_sends = [[], []]
    for half in (0, 1):
        for copy in ffn_gathers[half]:
            copy.wait_recv()
        block = slice(half * TP * HALF, (half + 1) * TP * HALF)
        hidden = jnp.maximum(dot(ffn_full[block, :], w_inner[...]), 0.0).astype(BF16)

        def project(peer):
            cols = pl.ds(pl.multiple_of(peer * width, width), width)
            partial[block, cols] = dot(hidden, w_outer[:, cols])
            partial[group_rows(half, tp), cols] += mixed_ref[half * HALF : (half + 1) * HALF, cols]
            return cols

        for offset in (2, 1, 3):
            peer = tp_peer(offset)
            cols = project(peer)
            send_cols[block, cols] = partial[block, cols].astype(BF16)
            copy = pltpu.make_async_remote_copy(
                src_ref=send_cols.at[block, cols],
                dst_ref=recv_cols.at[offset - 1, block, :],
                send_sem=rs2_send.at[half, offset - 1],
                recv_sem=rs2_recv.at[half, offset - 1],
                device_id={"tp": peer},
                device_id_type=MESH,
            )
            copy.start()
            col_sends[half].append(copy)
        project(tp)
    from_row = iota((tokens, tokens), 1)
    from_step = step_of(from_row // (TP * HALF) * HALF + from_row % HALF)
    source = (rep + REPLICAS * 2 - (from_row // HALF) % TP - TP * from_step) % REPLICAS
    restore = one_hot(iota((tokens, tokens), 0) == source)
    for copy in gathers + row_sends[0] + row_sends[1] + ffn_gathers[0] + ffn_gathers[1] + col_sends[0]:
        copy.wait_send()
    for slot in range(own):
        if slot != STAYS:
            deal(slot).wait_send()

    @pl.when(tp != 0)
    def _():
        deal(STAYS).wait_send()

    placed = jnp.zeros((tokens, width), F32)
    for half in (0, 1):
        block = slice(half * TP * HALF, (half + 1) * TP * HALF)
        for copy in col_sends[half]:
            copy.wait_recv()
        arrived = [recv_cols[i, block, :].astype(F32) for i in range(TP - 1)]
        final = partial[block, own_cols] + (arrived[0] + arrived[1] + arrived[2])
        placed += dot(restore[:, block], final.astype(BF16))
    out_ref[...] = placed.astype(BF16)
    for copy in col_sends[1]:
        copy.wait_send()


def on_device(
    tokens,
    attn_gain,
    ffn_gain,
    w_query,
    w_key,
    w_value,
    w_out,
    w_inner,
    w_outer,
    bias_table,
    cache_keys,
    cache_values,
    new_counts,
    cached_lengths,
    deal,
):
    rows, width = tokens.shape
    model = w_query.shape[0]
    ff = w_inner.shape[1]
    requests, cached, _ = cache_keys.shape
    slots = rows // requests
    heads = bias_table.shape[1]
    own = rows // TP
    hbm = pl.BlockSpec(memory_space=pltpu.HBM)
    vmem = pl.BlockSpec(memory_space=pltpu.VMEM)
    dma = pltpu.SemaphoreType.DMA
    return pl.pallas_call(
        kernel,
        out_shape=jax.ShapeDtypeStruct((rows, width), BF16),
        in_specs=[hbm] * 15,
        out_specs=vmem,
        scratch_shapes=[
            pltpu.VMEM((1, model), F32),
            pltpu.VMEM((1, model), F32),
            pltpu.SMEM((heads, BUCKETS), F32),
            pltpu.SMEM((requests,), jnp.int32),
            pltpu.SMEM((requests,), jnp.int32),
            pltpu.VMEM((1, rows), jnp.int32),
            pltpu.VMEM((rows, model), BF16),
            pltpu.VMEM((model, 3 * width), BF16),
            pltpu.VMEM((width, model), BF16),
            pltpu.VMEM((model, ff), BF16),
            pltpu.VMEM((ff, model), BF16),
            pltpu.VMEM((requests, cached, width), BF16),
            pltpu.VMEM((requests, cached, width), BF16),
            pltpu.VMEM((requests, heads * slots, cached + slots), F32),
            pltpu.VMEM((rows, model), F32),
            pltpu.VMEM((rows, model), BF16),
            pltpu.VMEM((2, TP - 1, HALF, model), BF16),
            pltpu.VMEM((rows, model), BF16),
            pltpu.VMEM((rows, model), BF16),
            pltpu.VMEM((TP - 1, rows, width), BF16),
            pltpu.VMEM((own, model), F32),
            pltpu.VMEM((own * LANES_OF_ROW, 128), F32),
            pltpu.VMEM((own, LANES_OF_ROW, 128), BF16),
            pltpu.VMEM((own, LANES_OF_ROW, 128), BF16),
            dma((15,)),
            dma((TP - 1,)),
            dma((TP - 1,)),
            dma((2, TP - 1)),
            dma((2, TP - 1)),
            dma((2, TP - 1)),
            dma((2, TP - 1)),
            dma((2, TP - 1)),
            dma((2, TP - 1)),
            dma((own,)),
            dma((own,)),
            pltpu.SemaphoreType.REGULAR,
            pltpu.SemaphoreType.REGULAR,
            pltpu.SemaphoreType.REGULAR,
        ],
        compiler_params=pltpu.CompilerParams(
            collective_id=0, has_side_effects=True, vmem_limit_bytes=40 * 1024 * 1024
        ),
    )(*[pltpu.with_memory_space_constraint(a, pltpu.HBM) for a in (
        tokens,
        attn_gain.reshape(1, model),
        ffn_gain.reshape(1, model),
        w_query,
        w_key,
        w_value,
        w_out,
        w_inner,
        w_outer,
        bias_table.T,
        cache_keys,
        cache_values,
        new_counts.reshape(requests),
        cached_lengths.reshape(requests),
        deal,
    )])


def solution(mesh):
    in_specs = (
        P("rep", "tp"),
        P(),
        P(),
        P(None, "tp"),
        P(None, "tp"),
        P(None, "tp"),
        P("tp", None),
        P(None, "tp"),
        P("tp", None),
        P(None, "tp"),
        P("rep", None, "tp"),
        P("rep", None, "tp"),
        P(None, "rep"),
        P(None, "rep"),
        P("rep", None),
    )
    out_specs = P("rep", "tp")
    return jax.shard_map(
        on_device, mesh=mesh, in_specs=in_specs, out_specs=out_specs, check_vma=False
    )
```

```python
import jax
import jax.numpy as jnp
from jax import lax
from jax.experimental import pallas as pl
from jax.experimental.pallas import tpu as pltpu
from jax.sharding import PartitionSpec as P

EPSILON = 1e-06
THRESHOLDS = (12, 16, 23, 32, 46, 64, 91)
BUCKETS = 32
TP = 4
REPLICAS = 128
SIDES = 8
DEPTH = 16
LANES_OF_ROW = 8
HALF = 16
NEAR = (1, 2, 14, 15)
MESH = pl.DeviceIdType.MESH
BF16 = jnp.bfloat16
F32 = jnp.float32


def iota(shape, dim):
    return lax.broadcasted_iota(jnp.int32, shape, dim)


def dot(a, b):
    return jnp.dot(a, b, preferred_element_type=F32)


def dot_t(a, b):
    return lax.dot_general(a, b, (((1,), (1,)), ((), ())), preferred_element_type=F32)


def bucket_of(relative):
    distance = jnp.abs(relative)
    larger = 8 + sum(((distance >= threshold).astype(jnp.int32) for threshold in THRESHOLDS))
    near = jnp.where(distance < 8, distance, larger)
    return near + 16 * (relative > 0).astype(jnp.int32)


def step_of(slot):
    return ((slot % HALF) // 4) * 8 + (slot % 4 + 6 + 4 * (slot // HALF)) % 8


STAYS = 2


def far_first(slots):
    return sorted(slots, key=lambda slot: -min(2 * step_of(slot) % DEPTH, -2 * step_of(slot) % DEPTH))


def one_hot(condition):
    return jnp.where(condition, 1.0, 0.0).astype(BF16)


def kernel(
    tokens_ref,
    attn_gain_hbm,
    ffn_gain_hbm,
    w_query_ref,
    w_key_ref,
    w_value_ref,
    w_out_ref,
    w_inner_ref,
    w_outer_ref,
    bias_hbm,
    cache_k_ref,
    cache_v_ref,
    counts_hbm,
    lengths_hbm,
    deal_hbm,
    out_ref,
    attn_gain_ref,
    ffn_gain_ref,
    bias_ref,
    counts_ref,
    lengths_ref,
    deal_ref,
    x_full,
    w_qkv,
    w_out,
    w_inner,
    w_outer,
    cache_k,
    cache_v,
    bias,
    partial,
    send_rows,
    recv_rows,
    ffn_full,
    send_cols,
    recv_cols,
    mixed_ref,
    slab,
    deal_send,
    deal_recv,
    load_sem,
    ag_send,
    ag_recv,
    rs_send,
    rs_recv,
    ag2_send,
    ag2_recv,
    rs2_send,
    rs2_recv,
    deal_send_sem,
    deal_recv_sem,
    relay_two,
    relay_four,
    relay_side,
):
    rep = lax.axis_index("rep")
    tp = lax.axis_index("tp")
    tokens, width = tokens_ref.shape
    model = w_qkv.shape[0]
    requests, cached, _ = cache_k_ref.shape
    slots = tokens // requests
    heads = bias_ref.shape[0]
    hdim = width // heads
    keys = cached + slots
    own = tokens // TP
    x_at, z_at, core = rep // (2 * DEPTH), (rep // 2) % DEPTH, rep % 2
    side = x_at * 2 + core

    def tp_peer(offset):
        return (tp + offset) % TP

    def side_peer(offset):
        other = (side + offset) % SIDES
        return (other // 2) * (2 * DEPTH) + z_at * 2 + other % 2

    def z_peer(offset):
        return x_at * (2 * DEPTH) + ((z_at + offset) % DEPTH) * 2 + core

    def greet(semaphore, peer):
        pl.semaphore_signal(semaphore, inc=1, device_id={"rep": peer}, device_id_type=MESH)

    barrier = pltpu.get_barrier_semaphore()
    for offset in range(1, TP):
        pl.semaphore_signal(barrier, inc=1, device_id={"tp": tp_peer(offset)}, device_id_type=MESH)
    for offset in range(1, SIDES):
        greet(barrier, side_peer(offset))
    for offset in NEAR:
        greet(barrier, z_peer(offset))

    own_cols = pl.ds(pl.multiple_of(tp * width, width), width)

    def group_rows(half, group):
        return pl.ds(pl.multiple_of((half * TP + group) * HALF, HALF), HALF)


    loads = [
        pltpu.make_async_copy(src, dst, load_sem.at[i])
        for i, (src, dst) in enumerate(
            [
                (tokens_ref, x_full.at[:, own_cols]),
                (bias_hbm, bias_ref),
                (counts_hbm, counts_ref),
                (lengths_hbm, lengths_ref),
                (deal_hbm, deal_ref),
                (attn_gain_hbm, attn_gain_ref),
                (ffn_gain_hbm, ffn_gain_ref),
                (w_query_ref, w_qkv.at[:, pl.ds(0, width)]),
                (w_key_ref, w_qkv.at[:, pl.ds(width, width)]),
                (w_value_ref, w_qkv.at[:, pl.ds(2 * width, width)]),
                (cache_k_ref, cache_k),
                (cache_v_ref, cache_v),
                (w_out_ref, w_out),
                (w_inner_ref, w_inner),
                (w_outer_ref, w_outer),
            ]
        )
    ]
    for load in loads:
        load.start()

    pl.semaphore_wait(barrier, (TP - 1) + (SIDES - 1) + len(NEAR))
    for offset in (2, DEPTH - 2):
        greet(relay_two, z_peer(offset))

    loads[0].wait()
    gathers = []
    for offset in (2, 1, 3):
        copy = pltpu.make_async_remote_copy(
            src_ref=x_full.at[:, own_cols],
            dst_ref=x_full.at[:, own_cols],
            send_sem=ag_send.at[offset - 1],
            recv_sem=ag_recv.at[offset - 1],
            device_id={"tp": tp_peer(offset)},
            device_id_type=MESH,
        )
        copy.start()
        gathers.append(copy)

    for load in loads[1:7]:
        load.wait()

    def squares_of(chunk):
        cols = pl.ds(pl.multiple_of(chunk * width, width), width)
        stream = x_full[:, cols].astype(F32)
        return jnp.sum(stream * stream, axis=1, keepdims=True)

    squares = squares_of(tp)

    key = iota((slots, keys), 1)
    query = iota((slots, keys), 0)
    for r in range(requests):
        length = lengths_ref[r]
        position = jnp.where(key < cached, key, length + key - cached)
        bucket = bucket_of(position - (length + query))
        rows = [jnp.zeros((slots, keys), F32) for _ in range(heads)]
        for b in range(BUCKETS):
            here = bucket == b
            rows = [jnp.where(here, bias_ref[h, b], rows[h]) for h in range(heads)]
        for h in range(heads):
            bias[r, pl.ds(h * slots, slots), :] = rows[h]

    q_row = iota((tokens, tokens), 0)
    k_col = iota((tokens, tokens), 1)
    q_group = (q_row // HALF) % TP
    q_step = step_of(q_row // (TP * HALF) * HALF + q_row % HALF)
    destination = (rep + q_group + TP * q_step) % REPLICAS
    count_of = jnp.where(k_col // slots == 0, counts_ref[0], counts_ref[requests - 1])
    live = (k_col % slots) < count_of
    order = jnp.where((deal_ref[...] == destination) & live, 1.0, 0.0)

    pl.semaphore_wait(relay_two, 2)
    for offset in (4, DEPTH - 4):
        greet(relay_four, z_peer(offset))

    for load in loads[7:10]:
        load.wait()
    for copy, offset in ((gathers[1], 1), (gathers[2], 3), (gathers[0], 2)):
        copy.wait_recv()
        squares += squares_of((tp + TP - offset) % TP)
    inverse = lax.rsqrt(squares / model + EPSILON)
    for c in range(TP):
        cols = slice(c * width, (c + 1) * width)
        send_rows[:, cols] = (x_full[:, cols].astype(F32) * inverse * attn_gain_ref[:, cols]).astype(BF16)
    qkv = dot(send_rows[...], w_qkv[...]).astype(BF16)

    loads[10].wait()
    loads[11].wait()
    lane_head = iota((slots, width), 1) // hdim
    key_row = iota((heads * slots, keys), 1)
    contexts = []
    for r in range(requests):
        rows = slice(r * slots, (r + 1) * slots)
        queries = qkv[rows, 0:width]
        all_keys = jnp.concatenate([cache_k[r], qkv[rows, width : 2 * width]], axis=0)
        all_values = jnp.concatenate([cache_v[r], qkv[rows, 2 * width :]], axis=0)
        stacked = jnp.concatenate(
            [jnp.where(lane_head == h, queries, jnp.zeros_like(queries)) for h in range(heads)], axis=0
        )
        scores = dot_t(stacked, all_keys) + bias[r]
        limit = jnp.where(key_row < cached, lengths_ref[r], cached + counts_ref[r])
        scores = jnp.where(key_row < limit, scores, -1e30)
        weights = jnp.exp(scores - jnp.max(scores, axis=1, keepdims=True))
        probs = (weights / jnp.sum(weights, axis=1, keepdims=True)).astype(BF16)
        spread = dot(probs, all_values)
        context = jnp.zeros((slots, width), F32)
        for h in range(heads):
            context = jnp.where(lane_head == h, spread[h * slots : (h + 1) * slots], context)
        contexts.append(context.astype(BF16))
    context = jnp.concatenate(contexts, axis=0)

    moved = dot(order.astype(BF16), context).astype(BF16)
    loads[12].wait()
    partial[...] = dot(moved, w_out[...])
    send_rows[...] = partial[...].astype(BF16)
    row_sends = [[], []]
    for half in (1, 0):
        for offset in (2, 1, 3):
            peer = tp_peer(offset)
            copy = pltpu.make_async_remote_copy(
                src_ref=send_rows.at[group_rows(half, peer), :],
                dst_ref=recv_rows.at[half, offset - 1],
                send_sem=rs_send.at[half, offset - 1],
                recv_sem=rs_recv.at[half, offset - 1],
                device_id={"tp": peer},
                device_id_type=MESH,
            )
            copy.start()
            row_sends[half].append(copy)

    pl.semaphore_wait(relay_four, 2)
    for offset in range(1, SIDES):
        greet(relay_side, side_peer(offset))

    own_q = iota((own, tokens), 0)
    own_k = iota((own, tokens), 1)
    own_destination = (rep + tp + TP * step_of(own_q)) % REPLICAS
    own_count = jnp.where(own_k // slots == 0, counts_ref[0], counts_ref[requests - 1])
    own_order = one_hot((deal_ref[...] == own_destination) & ((own_k % slots) < own_count))
    mixed_ref[...] = dot(own_order, x_full[...])

    def deal(slot):
        return pltpu.make_async_remote_copy(
            src_ref=deal_send.at[slot],
            dst_ref=deal_recv.at[slot],
            send_sem=deal_send_sem.at[slot],
            recv_sem=deal_recv_sem.at[slot],
            device_id={"rep": (rep + tp + TP * step_of(slot)) % REPLICAS},
            device_id_type=MESH,
        )

    stays = pltpu.make_async_copy(deal_send.at[STAYS], deal_recv.at[STAYS], deal_recv_sem.at[STAYS])
    lines = HALF * LANES_OF_ROW
    for half in (1, 0):
        for copy in row_sends[half]:
            copy.wait_recv()
        rows = slice(half * HALF, (half + 1) * HALF)
        arrived = [recv_rows[half, i].astype(F32) for i in range(TP - 1)]
        mixed = mixed_ref[rows, :] + partial[group_rows(half, tp), :] + (arrived[0] + arrived[1] + arrived[2])
        for c in range(LANES_OF_ROW):
            slab[pl.ds(half * lines + c, HALF, stride=LANES_OF_ROW), :] = mixed[:, c * 128 : (c + 1) * 128]
        deal_send[rows] = (
            slab[half * lines : (half + 1) * lines, :].reshape(HALF, LANES_OF_ROW, 128).astype(BF16)
        )
        if half == 1:
            pl.semaphore_wait(relay_side, SIDES - 1)
        for slot in far_first(range(half * HALF, (half + 1) * HALF)):
            if slot != STAYS:
                deal(slot).start()

    @pl.when(tp == 0)
    def _():
        stays.start()

    @pl.when(tp != 0)
    def _():
        deal(STAYS).start()

    ffn_gathers = [[], []]
    for half in (0, 1):
        rows = slice(half * HALF, (half + 1) * HALF)
        for slot in range(half * HALF, (half + 1) * HALF):
            if slot == STAYS:
                stays.wait()
            else:
                deal(slot).wait_recv()
        slab[half * lines : (half + 1) * lines, :] = deal_recv[rows].astype(F32).reshape(lines, 128)
        mixed = jnp.concatenate(
            [
                slab[pl.ds(half * lines + c, HALF, stride=LANES_OF_ROW), :]
                for c in range(LANES_OF_ROW)
            ],
            axis=1,
        )
        mixed_ref[rows, :] = mixed
        inverse_ffn = lax.rsqrt(jnp.mean(mixed * mixed, axis=1, keepdims=True) + EPSILON)
        ffn_full[group_rows(half, tp), :] = (mixed * inverse_ffn * ffn_gain_ref[...]).astype(BF16)
        for offset in (2, 1, 3):
            copy = pltpu.make_async_remote_copy(
                src_ref=ffn_full.at[group_rows(half, tp), :],
                dst_ref=ffn_full.at[group_rows(half, tp), :],
                send_sem=ag2_send.at[half, offset - 1],
                recv_sem=ag2_recv.at[half, offset - 1],
                device_id={"tp": tp_peer(offset)},
                device_id_type=MESH,
            )
            copy.start()
            ffn_gathers[half].append(copy)

    loads[13].wait()
    loads[14].wait()
    col_sends = [[], []]
    for half in (0, 1):
        for copy in ffn_gathers[half]:
            copy.wait_recv()
        block = slice(half * TP * HALF, (half + 1) * TP * HALF)
        hidden = jnp.maximum(dot(ffn_full[block, :], w_inner[...]), 0.0).astype(BF16)

        def project(peer):
            cols = pl.ds(pl.multiple_of(peer * width, width), width)
            partial[block, cols] = dot(hidden, w_outer[:, cols])
            partial[group_rows(half, tp), cols] += mixed_ref[half * HALF : (half + 1) * HALF, cols]
            return cols

        for offset in (2, 1, 3):
            peer = tp_peer(offset)
            cols = project(peer)
            send_cols[block, cols] = partial[block, cols].astype(BF16)
            copy = pltpu.make_async_remote_copy(
                src_ref=send_cols.at[block, cols],
                dst_ref=recv_cols.at[offset - 1, block, :],
                send_sem=rs2_send.at[half, offset - 1],
                recv_sem=rs2_recv.at[half, offset - 1],
                device_id={"tp": peer},
                device_id_type=MESH,
            )
            copy.start()
            col_sends[half].append(copy)
        project(tp)
    from_row = iota((tokens, tokens), 1)
    from_step = step_of(from_row // (TP * HALF) * HALF + from_row % HALF)
    source = (rep + REPLICAS * 2 - (from_row // HALF) % TP - TP * from_step) % REPLICAS
    restore = one_hot(iota((tokens, tokens), 0) == source)
    for copy in gathers + row_sends[0] + row_sends[1] + ffn_gathers[0] + ffn_gathers[1] + col_sends[0]:
        copy.wait_send()
    for slot in range(own):
        if slot != STAYS:
            deal(slot).wait_send()

    @pl.when(tp != 0)
    def _():
        deal(STAYS).wait_send()

    placed = jnp.zeros((tokens, width), F32)
    for half in (0, 1):
        block = slice(half * TP * HALF, (half + 1) * TP * HALF)
        for copy in col_sends[half]:
            copy.wait_recv()
        arrived = [recv_cols[i, block, :].astype(F32) for i in range(TP - 1)]
        final = partial[block, own_cols] + (arrived[0] + arrived[1] + arrived[2])
        placed += dot(restore[:, block], final.astype(BF16))
    out_ref[...] = placed.astype(BF16)
    for copy in col_sends[1]:
        copy.wait_send()


def on_device(
    tokens,
    attn_gain,
    ffn_gain,
    w_query,
    w_key,
    w_value,
    w_out,
    w_inner,
    w_outer,
    bias_table,
    cache_keys,
    cache_values,
    new_counts,
    cached_lengths,
    deal,
):
    rows, width = tokens.shape
    model = w_query.shape[0]
    ff = w_inner.shape[1]
    requests, cached, _ = cache_keys.shape
    slots = rows // requests
    heads = bias_table.shape[1]
    own = rows // TP
    hbm = pl.BlockSpec(memory_space=pltpu.HBM)
    vmem = pl.BlockSpec(memory_space=pltpu.VMEM)
    dma = pltpu.SemaphoreType.DMA
    return pl.pallas_call(
        kernel,
        out_shape=jax.ShapeDtypeStruct((rows, width), BF16),
        in_specs=[hbm] * 15,
        out_specs=vmem,
        scratch_shapes=[
            pltpu.VMEM((1, model), F32),
            pltpu.VMEM((1, model), F32),
            pltpu.SMEM((heads, BUCKETS), F32),
            pltpu.SMEM((requests,), jnp.int32),
            pltpu.SMEM((requests,), jnp.int32),
            pltpu.VMEM((1, rows), jnp.int32),
            pltpu.VMEM((rows, model), BF16),
            pltpu.VMEM((model, 3 * width), BF16),
            pltpu.VMEM((width, model), BF16),
            pltpu.VMEM((model, ff), BF16),
            pltpu.VMEM((ff, model), BF16),
            pltpu.VMEM((requests, cached, width), BF16),
            pltpu.VMEM((requests, cached, width), BF16),
            pltpu.VMEM((requests, heads * slots, cached + slots), F32),
            pltpu.VMEM((rows, model), F32),
            pltpu.VMEM((rows, model), BF16),
            pltpu.VMEM((2, TP - 1, HALF, model), BF16),
            pltpu.VMEM((rows, model), BF16),
            pltpu.VMEM((rows, model), BF16),
            pltpu.VMEM((TP - 1, rows, width), BF16),
            pltpu.VMEM((own, model), F32),
            pltpu.VMEM((own * LANES_OF_ROW + 8, 128), F32),
            pltpu.VMEM((own, LANES_OF_ROW, 128), BF16),
            pltpu.VMEM((own, LANES_OF_ROW, 128), BF16),
            dma((15,)),
            dma((TP - 1,)),
            dma((TP - 1,)),
            dma((2, TP - 1)),
            dma((2, TP - 1)),
            dma((2, TP - 1)),
            dma((2, TP - 1)),
            dma((2, TP - 1)),
            dma((2, TP - 1)),
            dma((own,)),
            dma((own,)),
            pltpu.SemaphoreType.REGULAR,
            pltpu.SemaphoreType.REGULAR,
            pltpu.SemaphoreType.REGULAR,
        ],
        compiler_params=pltpu.CompilerParams(
            collective_id=0, has_side_effects=True, vmem_limit_bytes=40 * 1024 * 1024
        ),
    )(*[pltpu.with_memory_space_constraint(a, pltpu.HBM) for a in (
        tokens,
        attn_gain.reshape(1, model),
        ffn_gain.reshape(1, model),
        w_query,
        w_key,
        w_value,
        w_out,
        w_inner,
        w_outer,
        bias_table.T,
        cache_keys,
        cache_values,
        new_counts.reshape(requests),
        cached_lengths.reshape(requests),
        deal,
    )])


def solution(mesh):
    in_specs = (
        P("rep", "tp"),
        P(),
        P(),
        P(None, "tp"),
        P(None, "tp"),
        P(None, "tp"),
        P("tp", None),
        P(None, "tp"),
        P("tp", None),
        P(None, "tp"),
        P("rep", None, "tp"),
        P("rep", None, "tp"),
        P(None, "rep"),
        P(None, "rep"),
        P("rep", None),
    )
    out_specs = P("rep", "tp")
    return jax.shard_map(
        on_device, mesh=mesh, in_specs=in_specs, out_specs=out_specs, check_vma=False
    )
```

```python
import jax
import jax.numpy as jnp
from jax import lax
from jax.experimental import pallas as pl
from jax.experimental.pallas import tpu as pltpu
from jax.sharding import PartitionSpec as P

EPSILON = 1e-06
THRESHOLDS = (12, 16, 23, 32, 46, 64, 91)
BUCKETS = 32
TP = 4
REPLICAS = 128
SIDES = 8
DEPTH = 16
LANES_OF_ROW = 8
HALF = 16
NEAR = (1, 2, 14, 15)
MESH = pl.DeviceIdType.MESH
BF16 = jnp.bfloat16
F32 = jnp.float32


def iota(shape, dim):
    return lax.broadcasted_iota(jnp.int32, shape, dim)


def dot(a, b):
    return jnp.dot(a, b, preferred_element_type=F32)


def dot_t(a, b):
    return lax.dot_general(a, b, (((1,), (1,)), ((), ())), preferred_element_type=F32)


def bucket_of(relative):
    distance = jnp.abs(relative)
    larger = 8 + sum(((distance >= threshold).astype(jnp.int32) for threshold in THRESHOLDS))
    near = jnp.where(distance < 8, distance, larger)
    return near + 16 * (relative > 0).astype(jnp.int32)


def step_of(slot):
    return ((slot % HALF) // 4) * 8 + (slot % 4 + 6 + 4 * (slot // HALF)) % 8


STAYS = 2


def far_first(slots):
    return sorted(slots, key=lambda slot: -min(2 * step_of(slot) % DEPTH, -2 * step_of(slot) % DEPTH))


def one_hot(condition):
    return jnp.where(condition, 1.0, 0.0).astype(BF16)


def kernel(
    tokens_ref,
    attn_gain_hbm,
    ffn_gain_hbm,
    w_query_ref,
    w_key_ref,
    w_value_ref,
    w_out_ref,
    w_inner_ref,
    w_outer_ref,
    bias_hbm,
    cache_k_ref,
    cache_v_ref,
    counts_hbm,
    lengths_hbm,
    deal_hbm,
    out_ref,
    attn_gain_ref,
    ffn_gain_ref,
    bias_ref,
    counts_ref,
    lengths_ref,
    deal_ref,
    x_full,
    w_qkv,
    w_out,
    w_inner,
    w_outer,
    cache_k,
    cache_v,
    bias,
    partial,
    send_rows,
    recv_rows,
    ffn_full,
    send_cols,
    recv_cols,
    mixed_ref,
    slab,
    deal_send,
    deal_recv,
    load_sem,
    ag_send,
    ag_recv,
    rs_send,
    rs_recv,
    ag2_send,
    ag2_recv,
    rs2_send,
    rs2_recv,
    deal_send_sem,
    deal_recv_sem,
    relay_two,
    relay_four,
    relay_side,
):
    rep = lax.axis_index("rep")
    tp = lax.axis_index("tp")
    tokens, width = tokens_ref.shape
    model = w_qkv.shape[0]
    requests, cached, _ = cache_k_ref.shape
    slots = tokens // requests
    heads = bias_ref.shape[0]
    hdim = width // heads
    keys = cached + slots
    own = tokens // TP
    x_at, z_at, core = rep // (2 * DEPTH), (rep // 2) % DEPTH, rep % 2
    side = x_at * 2 + core

    def tp_peer(offset):
        return (tp + offset) % TP

    def side_peer(offset):
        other = (side + offset) % SIDES
        return (other // 2) * (2 * DEPTH) + z_at * 2 + other % 2

    def z_peer(offset):
        return x_at * (2 * DEPTH) + ((z_at + offset) % DEPTH) * 2 + core

    def greet(semaphore, peer):
        pl.semaphore_signal(semaphore, inc=1, device_id={"rep": peer}, device_id_type=MESH)

    barrier = pltpu.get_barrier_semaphore()
    for offset in range(1, TP):
        pl.semaphore_signal(barrier, inc=1, device_id={"tp": tp_peer(offset)}, device_id_type=MESH)
    for offset in range(1, SIDES):
        greet(barrier, side_peer(offset))
    for offset in NEAR:
        greet(barrier, z_peer(offset))

    own_cols = pl.ds(pl.multiple_of(tp * width, width), width)

    def group_rows(half, group):
        return pl.ds(pl.multiple_of((half * TP + group) * HALF, HALF), HALF)


    loads = [
        pltpu.make_async_copy(src, dst, load_sem.at[i])
        for i, (src, dst) in enumerate(
            [
                (tokens_ref, x_full.at[:, own_cols]),
                (bias_hbm, bias_ref),
                (counts_hbm, counts_ref),
                (lengths_hbm, lengths_ref),
                (deal_hbm, deal_ref),
                (attn_gain_hbm, attn_gain_ref),
                (ffn_gain_hbm, ffn_gain_ref),
                (w_query_ref, w_qkv.at[:, pl.ds(0, width)]),
                (w_key_ref, w_qkv.at[:, pl.ds(width, width)]),
                (w_value_ref, w_qkv.at[:, pl.ds(2 * width, width)]),
                (cache_k_ref, cache_k),
                (cache_v_ref, cache_v),
                (w_out_ref, w_out),
                (w_inner_ref, w_inner),
                (w_outer_ref, w_outer),
            ]
        )
    ]
    for load in loads:
        load.start()

    pl.semaphore_wait(barrier, (TP - 1) + (SIDES - 1) + len(NEAR))
    for offset in (2, DEPTH - 2):
        greet(relay_two, z_peer(offset))

    loads[0].wait()
    gathers = []
    for offset in (2, 1, 3):
        copy = pltpu.make_async_remote_copy(
            src_ref=x_full.at[:, own_cols],
            dst_ref=x_full.at[:, own_cols],
            send_sem=ag_send.at[offset - 1],
            recv_sem=ag_recv.at[offset - 1],
            device_id={"tp": tp_peer(offset)},
            device_id_type=MESH,
        )
        copy.start()
        gathers.append(copy)

    for load in loads[1:7]:
        load.wait()

    def squares_of(chunk):
        cols = pl.ds(pl.multiple_of(chunk * width, width), width)
        stream = x_full[:, cols].astype(F32)
        return jnp.sum(stream * stream, axis=1, keepdims=True)

    squares = squares_of(tp)

    key = iota((slots, keys), 1)
    query = iota((slots, keys), 0)
    for r in range(requests):
        length = lengths_ref[r]
        position = jnp.where(key < cached, key, length + key - cached)
        bucket = bucket_of(position - (length + query))
        rows = [jnp.zeros((slots, keys), F32) for _ in range(heads)]
        for b in range(BUCKETS):
            here = bucket == b
            rows = [jnp.where(here, bias_ref[h, b], rows[h]) for h in range(heads)]
        for h in range(heads):
            bias[r, pl.ds(h * slots, slots), :] = rows[h]

    q_row = iota((tokens, tokens), 0)
    k_col = iota((tokens, tokens), 1)
    q_group = (q_row // HALF) % TP
    q_step = step_of(q_row // (TP * HALF) * HALF + q_row % HALF)
    destination = (rep + q_group + TP * q_step) % REPLICAS
    count_of = jnp.where(k_col // slots == 0, counts_ref[0], counts_ref[requests - 1])
    live = (k_col % slots) < count_of
    order = jnp.where((deal_ref[...] == destination) & live, 1.0, 0.0)

    pl.semaphore_wait(relay_two, 2)
    for offset in (4, DEPTH - 4):
        greet(relay_four, z_peer(offset))

    for load in loads[7:10]:
        load.wait()
    for copy, offset in ((gathers[1], 1), (gathers[2], 3), (gathers[0], 2)):
        copy.wait_recv()
        squares += squares_of((tp + TP - offset) % TP)
    inverse = lax.rsqrt(squares / model + EPSILON)
    for c in range(TP):
        cols = slice(c * width, (c + 1) * width)
        send_rows[:, cols] = (x_full[:, cols].astype(F32) * inverse * attn_gain_ref[:, cols]).astype(BF16)
    qkv = dot(send_rows[...], w_qkv[...]).astype(BF16)

    loads[10].wait()
    loads[11].wait()
    lane_head = iota((slots, width), 1) // hdim
    key_row = iota((heads * slots, keys), 1)
    contexts = []
    for r in range(requests):
        rows = slice(r * slots, (r + 1) * slots)
        queries = qkv[rows, 0:width]
        all_keys = jnp.concatenate([cache_k[r], qkv[rows, width : 2 * width]], axis=0)
        all_values = jnp.concatenate([cache_v[r], qkv[rows, 2 * width :]], axis=0)
        stacked = jnp.concatenate(
            [jnp.where(lane_head == h, queries, jnp.zeros_like(queries)) for h in range(heads)], axis=0
        )
        scores = dot_t(stacked, all_keys) + bias[r]
        limit = jnp.where(key_row < cached, lengths_ref[r], cached + counts_ref[r])
        scores = jnp.where(key_row < limit, scores, -1e30)
        weights = jnp.exp(scores - jnp.max(scores, axis=1, keepdims=True))
        probs = (weights / jnp.sum(weights, axis=1, keepdims=True)).astype(BF16)
        spread = dot(probs, all_values)
        context = jnp.zeros((slots, width), F32)
        for h in range(heads):
            context = jnp.where(lane_head == h, spread[h * slots : (h + 1) * slots], context)
        contexts.append(context.astype(BF16))
    context = jnp.concatenate(contexts, axis=0)

    moved = dot(order.astype(BF16), context).astype(BF16)
    loads[12].wait()
    row_sends = [[], []]
    for half in (1, 0):
        block = slice(half * TP * HALF, (half + 1) * TP * HALF)
        partial[block, :] = dot(moved[block], w_out[...])
        send_rows[block, :] = partial[block, :].astype(BF16)
        for offset in (2, 1, 3):
            peer = tp_peer(offset)
            copy = pltpu.make_async_remote_copy(
                src_ref=send_rows.at[group_rows(half, peer), :],
                dst_ref=recv_rows.at[half, offset - 1],
                send_sem=rs_send.at[half, offset - 1],
                recv_sem=rs_recv.at[half, offset - 1],
                device_id={"tp": peer},
                device_id_type=MESH,
            )
            copy.start()
            row_sends[half].append(copy)

    pl.semaphore_wait(relay_four, 2)
    for offset in range(1, SIDES):
        greet(relay_side, side_peer(offset))

    own_q = iota((own, tokens), 0)
    own_k = iota((own, tokens), 1)
    own_destination = (rep + tp + TP * step_of(own_q)) % REPLICAS
    own_count = jnp.where(own_k // slots == 0, counts_ref[0], counts_ref[requests - 1])
    own_order = one_hot((deal_ref[...] == own_destination) & ((own_k % slots) < own_count))
    mixed_ref[...] = dot(own_order, x_full[...])

    def deal(slot):
        return pltpu.make_async_remote_copy(
            src_ref=deal_send.at[slot],
            dst_ref=deal_recv.at[slot],
            send_sem=deal_send_sem.at[slot],
            recv_sem=deal_recv_sem.at[slot],
            device_id={"rep": (rep + tp + TP * step_of(slot)) % REPLICAS},
            device_id_type=MESH,
        )

    stays = pltpu.make_async_copy(deal_send.at[STAYS], deal_recv.at[STAYS], deal_recv_sem.at[STAYS])
    lines = HALF * LANES_OF_ROW
    for half in (1, 0):
        for copy in row_sends[half]:
            copy.wait_recv()
        rows = slice(half * HALF, (half + 1) * HALF)
        arrived = [recv_rows[half, i].astype(F32) for i in range(TP - 1)]
        mixed = mixed_ref[rows, :] + partial[group_rows(half, tp), :] + (arrived[0] + arrived[1] + arrived[2])
        for c in range(LANES_OF_ROW):
            slab[pl.ds(half * lines + c, HALF, stride=LANES_OF_ROW), :] = mixed[:, c * 128 : (c + 1) * 128]
        deal_send[rows] = (
            slab[half * lines : (half + 1) * lines, :].reshape(HALF, LANES_OF_ROW, 128).astype(BF16)
        )
        if half == 1:
            pl.semaphore_wait(relay_side, SIDES - 1)
        for slot in far_first(range(half * HALF, (half + 1) * HALF)):
            if slot != STAYS:
                deal(slot).start()

    @pl.when(tp == 0)
    def _():
        stays.start()

    @pl.when(tp != 0)
    def _():
        deal(STAYS).start()

    ffn_gathers = [[], []]
    for half in (0, 1):
        rows = slice(half * HALF, (half + 1) * HALF)
        for slot in range(half * HALF, (half + 1) * HALF):
            if slot == STAYS:
                stays.wait()
            else:
                deal(slot).wait_recv()
        slab[half * lines : (half + 1) * lines, :] = deal_recv[rows].astype(F32).reshape(lines, 128)
        mixed = jnp.concatenate(
            [
                slab[pl.ds(half * lines + c, HALF, stride=LANES_OF_ROW), :]
                for c in range(LANES_OF_ROW)
            ],
            axis=1,
        )
        mixed_ref[rows, :] = mixed
        inverse_ffn = lax.rsqrt(jnp.mean(mixed * mixed, axis=1, keepdims=True) + EPSILON)
        ffn_full[group_rows(half, tp), :] = (mixed * inverse_ffn * ffn_gain_ref[...]).astype(BF16)
        for offset in (2, 1, 3):
            copy = pltpu.make_async_remote_copy(
                src_ref=ffn_full.at[group_rows(half, tp), :],
                dst_ref=ffn_full.at[group_rows(half, tp), :],
                send_sem=ag2_send.at[half, offset - 1],
                recv_sem=ag2_recv.at[half, offset - 1],
                device_id={"tp": tp_peer(offset)},
                device_id_type=MESH,
            )
            copy.start()
            ffn_gathers[half].append(copy)

    loads[13].wait()
    loads[14].wait()
    col_sends = [[], []]
    for half in (0, 1):
        for copy in ffn_gathers[half]:
            copy.wait_recv()
        block = slice(half * TP * HALF, (half + 1) * TP * HALF)
        hidden = jnp.maximum(dot(ffn_full[block, :], w_inner[...]), 0.0).astype(BF16)

        def project(peer):
            cols = pl.ds(pl.multiple_of(peer * width, width), width)
            partial[block, cols] = dot(hidden, w_outer[:, cols])
            partial[group_rows(half, tp), cols] += mixed_ref[half * HALF : (half + 1) * HALF, cols]
            return cols

        for offset in (2, 1, 3):
            peer = tp_peer(offset)
            cols = project(peer)
            send_cols[block, cols] = partial[block, cols].astype(BF16)
            copy = pltpu.make_async_remote_copy(
                src_ref=send_cols.at[block, cols],
                dst_ref=recv_cols.at[offset - 1, block, :],
                send_sem=rs2_send.at[half, offset - 1],
                recv_sem=rs2_recv.at[half, offset - 1],
                device_id={"tp": peer},
                device_id_type=MESH,
            )
            copy.start()
            col_sends[half].append(copy)
        project(tp)
    from_row = iota((tokens, tokens), 1)
    from_step = step_of(from_row // (TP * HALF) * HALF + from_row % HALF)
    source = (rep + REPLICAS * 2 - (from_row // HALF) % TP - TP * from_step) % REPLICAS
    restore = one_hot(iota((tokens, tokens), 0) == source)
    for copy in gathers + row_sends[0] + row_sends[1] + ffn_gathers[0] + ffn_gathers[1] + col_sends[0]:
        copy.wait_send()
    for slot in range(own):
        if slot != STAYS:
            deal(slot).wait_send()

    @pl.when(tp != 0)
    def _():
        deal(STAYS).wait_send()

    placed = jnp.zeros((tokens, width), F32)
    for half in (0, 1):
        block = slice(half * TP * HALF, (half + 1) * TP * HALF)
        for copy in col_sends[half]:
            copy.wait_recv()
        arrived = [recv_cols[i, block, :].astype(F32) for i in range(TP - 1)]
        final = partial[block, own_cols] + (arrived[0] + arrived[1] + arrived[2])
        placed += dot(restore[:, block], final.astype(BF16))
    out_ref[...] = placed.astype(BF16)
    for copy in col_sends[1]:
        copy.wait_send()


def on_device(
    tokens,
    attn_gain,
    ffn_gain,
    w_query,
    w_key,
    w_value,
    w_out,
    w_inner,
    w_outer,
    bias_table,
    cache_keys,
    cache_values,
    new_counts,
    cached_lengths,
    deal,
):
    rows, width = tokens.shape
    model = w_query.shape[0]
    ff = w_inner.shape[1]
    requests, cached, _ = cache_keys.shape
    slots = rows // requests
    heads = bias_table.shape[1]
    own = rows // TP
    hbm = pl.BlockSpec(memory_space=pltpu.HBM)
    vmem = pl.BlockSpec(memory_space=pltpu.VMEM)
    dma = pltpu.SemaphoreType.DMA
    return pl.pallas_call(
        kernel,
        out_shape=jax.ShapeDtypeStruct((rows, width), BF16),
        in_specs=[hbm] * 15,
        out_specs=vmem,
        scratch_shapes=[
            pltpu.VMEM((1, model), F32),
            pltpu.VMEM((1, model), F32),
            pltpu.SMEM((heads, BUCKETS), F32),
            pltpu.SMEM((requests,), jnp.int32),
            pltpu.SMEM((requests,), jnp.int32),
            pltpu.VMEM((1, rows), jnp.int32),
            pltpu.VMEM((rows, model), BF16),
            pltpu.VMEM((model, 3 * width), BF16),
            pltpu.VMEM((width, model), BF16),
            pltpu.VMEM((model, ff), BF16),
            pltpu.VMEM((ff, model), BF16),
            pltpu.VMEM((requests, cached, width), BF16),
            pltpu.VMEM((requests, cached, width), BF16),
            pltpu.VMEM((requests, heads * slots, cached + slots), F32),
            pltpu.VMEM((rows, model), F32),
            pltpu.VMEM((rows, model), BF16),
            pltpu.VMEM((2, TP - 1, HALF, model), BF16),
            pltpu.VMEM((rows, model), BF16),
            pltpu.VMEM((rows, model), BF16),
            pltpu.VMEM((TP - 1, rows, width), BF16),
            pltpu.VMEM((own, model), F32),
            pltpu.VMEM((own * LANES_OF_ROW, 128), F32),
            pltpu.VMEM((own, LANES_OF_ROW, 128), BF16),
            pltpu.VMEM((own, LANES_OF_ROW, 128), BF16),
            dma((15,)),
            dma((TP - 1,)),
            dma((TP - 1,)),
            dma((2, TP - 1)),
            dma((2, TP - 1)),
            dma((2, TP - 1)),
            dma((2, TP - 1)),
            dma((2, TP - 1)),
            dma((2, TP - 1)),
            dma((own,)),
            dma((own,)),
            pltpu.SemaphoreType.REGULAR,
            pltpu.SemaphoreType.REGULAR,
            pltpu.SemaphoreType.REGULAR,
        ],
        compiler_params=pltpu.CompilerParams(
            collective_id=0, has_side_effects=True, vmem_limit_bytes=40 * 1024 * 1024
        ),
    )(*[pltpu.with_memory_space_constraint(a, pltpu.HBM) for a in (
        tokens,
        attn_gain.reshape(1, model),
        ffn_gain.reshape(1, model),
        w_query,
        w_key,
        w_value,
        w_out,
        w_inner,
        w_outer,
        bias_table.T,
        cache_keys,
        cache_values,
        new_counts.reshape(requests),
        cached_lengths.reshape(requests),
        deal,
    )])


def solution(mesh):
    in_specs = (
        P("rep", "tp"),
        P(),
        P(),
        P(None, "tp"),
        P(None, "tp"),
        P(None, "tp"),
        P("tp", None),
        P(None, "tp"),
        P("tp", None),
        P(None, "tp"),
        P("rep", None, "tp"),
        P("rep", None, "tp"),
        P(None, "rep"),
        P(None, "rep"),
        P("rep", None),
    )
    out_specs = P("rep", "tp")
    return jax.shard_map(
        on_device, mesh=mesh, in_specs=in_specs, out_specs=out_specs, check_vma=False
    )
```
